256 devices in a mesh: seq: 32 (over x, y, core), pipe: 8 (over z).
Axes of the slice: x: 4, y: 4, z: 8, core: 2. Of those that a mesh axis runs over, the one named last changes fastest.
Arguments:
- section_inputs: bfloat16 [8, 4096, 1536], P('pipe', 'seq'), may hold values from -6 to 6
- cotangent: bfloat16 [4096, 1536], P('seq'), may hold values from -6 to 6
- gain: float32 [8, 1536], P('pipe'), may hold values from 0.25 to 1.75
- w_gate: bfloat16 [8, 1536, 1536], P('pipe'), may hold values from -0.15625 to 0.15625
- w_out: bfloat16 [8, 1536, 1536], P('pipe'), may hold values from -0.15625 to 0.15625
- mix_first: bfloat16 [8, 64, 64, 64], P('pipe', 'seq'), may hold values from -0.75 to 0.75
- mix_second: bfloat16 [8, 64, 64, 64], P('pipe', 'seq'), may hold values from -0.75 to 0.75
Outputs:
- grad_inputs: bfloat16 [8, 4096, 1536], P('pipe', 'seq')
- grad_first: float32 [8, 64, 64, 64], P('pipe', 'seq')
- grad_second: float32 [8, 64, 64, 64], P('pipe', 'seq')
The draws below stay inside these ranges and needn't reach their ends.
All inputs are finite; a program needn't handle non-finite values.
Results may differ from the reference program's by a relative error of at most 0.025.
Values may be sent and summed in bfloat16 or wider, within the bound.
A program may use at most 64 MiB of HBM per device.

```python
import jax
import jax.numpy as jnp
from jax import lax

D = 1536
BLOCK = 64
LAYERS = 8
TOKENS = 4096
BLOCKS = 64
N_PIPE = 8


def block_scale(stream_key, extent, cuts, low, top_value):
    def one(position, shards_of):
        steps = jax.random.uniform(jax.random.fold_in(jax.random.fold_in(stream_key, 6), position), (shards_of,), jnp.float32, low / len(cuts), top_value / len(cuts))
        return jnp.repeat(jnp.exp(steps), extent[position] // shards_of).reshape((-1,) + (1,) * (len(extent) - position - 1))

    factor_of = one(*cuts[0])
    for cut in cuts[1:]:
        factor_of = factor_of * one(*cut)
    return factor_of


def normal_values(stream_key, shape, width, bound, pieces=(), dtype=jnp.bfloat16):
    level = block_scale(stream_key, shape, pieces, -0.22, 0.18) if pieces else 1.0
    result = jax.random.normal(stream_key, shape, jnp.float32) * width * level
    return jnp.minimum(jnp.maximum(result, -bound), bound).astype(dtype)


def setup_inputs(seed: int = 0) -> dict:
    key_of = jax.random.split(jax.random.key(seed), 8)
    section_inputs = normal_values(key_of[0], (LAYERS, TOKENS, D), 1.0, 6.0, ((0, 8), (1, 32)))
    cotangent = normal_values(key_of[1], (TOKENS, D), 1.0, 6.0, ((0, 32),))
    gain = jnp.clip(1.0 + 0.15 * jax.random.normal(key_of[2], (LAYERS, D), jnp.float32), 0.25, 1.75)
    w_gate = normal_values(key_of[3], (LAYERS, D, D), D ** -0.5, 0.15625, ((0, 8),))
    w_out = normal_values(key_of[4], (LAYERS, D, D), D ** -0.5, 0.15625, ((0, 8),))
    mix_first = normal_values(key_of[5], (LAYERS, BLOCKS, BLOCK, BLOCK), BLOCK ** -0.5, 0.75, ((0, 8), (1, 32)))
    mix_second = normal_values(key_of[6], (LAYERS, BLOCKS, BLOCK, BLOCK), BLOCK ** -0.5, 0.75, ((0, 8), (1, 32)))
    return {"section_inputs": section_inputs, "cotangent": cotangent, "gain": gain, "w_gate": w_gate, "w_out": w_out, "mix_first": mix_first, "mix_second": mix_second}


def layer_grad(inputs, incoming, gain_row, weight_gate, weight_out, first_blocks, second_blocks):
    features = inputs.astype(jnp.float32)
    inv_rms = lax.rsqrt(lax.optimization_barrier(jnp.mean(features * features, axis=-1, keepdims=True)) + 1e-06)
    unit_rows = features * inv_rms
    normed = (unit_rows * gain_row).astype(jnp.bfloat16)
    normed_blocks = normed.reshape(BLOCKS, BLOCK, D)
    first_out = jnp.einsum('kij,kjc->kic', first_blocks.astype(jnp.float32), normed_blocks.astype(jnp.float32)).astype(jnp.bfloat16)
    moved_blocks = jnp.transpose(first_out, (1, 0, 2)).reshape(BLOCKS, BLOCK, D)
    mixer_out = jnp.einsum('kij,kjc->kic', second_blocks.astype(jnp.float32), moved_blocks.astype(jnp.float32)).reshape(TOKENS, D)
    gate_pre = jnp.dot(normed, weight_gate, preferred_element_type=jnp.float32)
    sigma = jax.nn.sigmoid(gate_pre)
    delta_hidden = jnp.dot(incoming, weight_out.T, preferred_element_type=jnp.float32)
    delta_mix = (delta_hidden * gate_pre * sigma).astype(jnp.bfloat16)
    delta_gate = (delta_hidden * mixer_out * sigma * (1.0 + gate_pre * (1.0 - sigma))).astype(jnp.bfloat16)
    mix_blocks = delta_mix.reshape(BLOCKS, BLOCK, D)
    delta_moved = jnp.einsum('kij,kic->kjc', second_blocks.astype(jnp.float32), mix_blocks.astype(jnp.float32)).astype(jnp.bfloat16)
    delta_mid = jnp.transpose(delta_moved.reshape(BLOCK, BLOCKS, D), (1, 0, 2))
    first_back = jnp.einsum('kij,kic->kjc', first_blocks.astype(jnp.float32), delta_mid.astype(jnp.float32)).reshape(TOKENS, D)
    gate_back = jnp.dot(delta_gate, weight_gate.T, preferred_element_type=jnp.float32)
    delta_norm = (first_back + gate_back) * gain_row
    centred = delta_norm - unit_rows * lax.optimization_barrier(jnp.mean(delta_norm * unit_rows, axis=-1, keepdims=True))
    outgoing = (incoming.astype(jnp.float32) + inv_rms * centred).astype(jnp.bfloat16)
    grad_first_layer = jnp.einsum('kic,kjc->kij', delta_mid.astype(jnp.float32), normed_blocks.astype(jnp.float32))
    grad_second_layer = jnp.einsum('kic,kjc->kij', mix_blocks.astype(jnp.float32), moved_blocks.astype(jnp.float32))
    return (outgoing, grad_first_layer, grad_second_layer)

def reference(section_inputs, cotangent, gain, w_gate, w_out, mix_first, mix_second):
    incoming = cotangent
    input_grads = []
    first_grads = []
    second_grads = []
    for layer_index in reversed(range(N_PIPE)):
        outgoing, grad_first_layer, grad_second_layer = layer_grad(section_inputs[layer_index], incoming, gain[layer_index], w_gate[layer_index], w_out[layer_index], mix_first[layer_index], mix_second[layer_index])
        input_grads.insert(0, outgoing)
        first_grads.insert(0, grad_first_layer)
        second_grads.insert(0, grad_second_layer)
        incoming = outgoing
    return (jnp.stack(input_grads), jnp.stack(first_grads), jnp.stack(second_grads))
```

```python
import functools

import jax
import jax.numpy as jnp
from jax import lax
from jax.experimental import pallas as pl
from jax.experimental.pallas import tpu as pltpu
from jax.sharding import PartitionSpec as P

MESH = pl.DeviceIdType.MESH
F32 = jnp.float32
BF16 = jnp.bfloat16
LANES = 128
CUTS = 4
CHUNK = LANES * CUTS
ROWS_TO = 4
PIECE = ROWS_TO * CUTS


def iota(shape, axis):
    return lax.broadcasted_iota(jnp.int32, shape, axis)


def dot(a, b, da=1, db=0):
    return lax.dot_general(a, b, (((da,), (db,)), ((), ())), preferred_element_type=F32)


def as_bf16(mask):
    return jnp.where(mask, 1.0, 0.0).astype(BF16)


def kernel(
    n_seq,
    n_pipe,
    x_hbm,
    cot_hbm,
    gain_hbm,
    wg_hbm,
    wo_hbm,
    m1_hbm,
    m2_hbm,
    out_ref,
    g1_ref,
    g2_ref,
    x,
    gain,
    wg,
    wo,
    m1,
    m2,
    xnext,
    xw,
    inv,
    shift,
    nrm,
    nst,
    dfwd,
    efwd,
    dbwd,
    ebwd,
    pick1,
    pick2,
    fsend,
    frecv,
    bsend,
    brecv,
    moved,
    mf,
    gf,
    dh,
    dmix,
    dgate,
    gb,
    anat,
    asend,
    arecv,
    csend,
    crecv,
    lsem,
    xs_sem,
    xr_sem,
    fs_sem,
    fr_sem,
    bs_sem,
    br_sem,
    zs_sem,
    zr_sem,
    cs_sem,
    cr_sem,
):
    me = lax.axis_index("seq")
    section = lax.axis_index("pipe")
    rows, width = x.shape
    block = rows // 2
    chunks = width // CHUNK
    span = n_seq * PIECE
    first = section == n_pipe - 1
    last = section == 0
    before = lax.rem(section + n_pipe - 1, n_pipe)
    after = lax.rem(section + 1, n_pipe)

    loads = [
        pltpu.make_async_copy(src, dst, lsem.at[i])
        for i, (src, dst) in enumerate(
            ((x_hbm, x), (m1_hbm, m1), (m2_hbm, m2), (gain_hbm, gain), (wg_hbm, wg), (wo_hbm, wo))
        )
    ]
    for copy in loads:
        copy.start()

    def cot_copy(f):
        return pltpu.make_async_copy(
            cot_hbm.at[:, f * CHUNK : (f + 1) * CHUNK], arecv.at[f], zr_sem.at[f]
        )

    @pl.when(first)
    def _():
        for f in range(chunks):
            cot_copy(f).start()

    barrier = pltpu.get_barrier_semaphore()

    @pl.loop(1, n_seq)
    def _(i):
        pl.semaphore_signal(
            barrier, inc=1, device_id={"seq": lax.rem(me + i, n_seq)}, device_id_type=MESH
        )

    pl.semaphore_signal(barrier, inc=1, device_id={"pipe": before}, device_id_type=MESH)
    pl.semaphore_signal(barrier, inc=1, device_id={"pipe": after}, device_id_type=MESH)

    loads[1].wait()
    loads[2].wait()

    def diagonal(blocks):
        spread = as_bf16(iota((block, rows), 0) == iota((block, rows), 1) % block)
        wide = dot(blocks, spread)
        same = iota((rows, rows), 0) // block == iota((rows, rows), 1) // block
        return jnp.where(same, wide, 0.0).astype(BF16)

    d1 = diagonal(m1[...])
    d2 = diagonal(m2[...])
    spot = iota((span, rows), 0)
    col = iota((span, rows), 1)
    dest = spot // PIECE
    quad = spot % ROWS_TO
    sel1 = as_bf16(col == (quad % 2) * block + dest * 2 + quad // 2)
    sel2 = as_bf16(col == (quad // 2) * block + dest * 2 + quad % 2)
    spot_t = iota((rows, span), 1)
    row_t = iota((rows, span), 0)
    dest_t = spot_t // PIECE
    quad_t = spot_t % ROWS_TO
    sel1_t = as_bf16(row_t == (quad_t % 2) * block + dest_t * 2 + quad_t // 2)
    sel2_t = as_bf16(row_t == (quad_t // 2) * block + dest_t * 2 + quad_t % 2)
    tall = ((dfwd, dot(sel1, d1)), (dbwd, dot(sel2, d2, 1, 1)))
    cut_of = (spot // ROWS_TO) % CUTS
    for ref, value in tall:
        for c in range(CUTS):
            ref[:, c * rows : (c + 1) * rows] = jnp.where(cut_of == c, value, 0.0).astype(BF16)
    flat = (
        (efwd, dot(d2, sel2_t)),
        (ebwd, dot(d1, sel1_t, 0, 0)),
        (pick1, sel1_t.astype(F32)),
        (pick2, sel2_t.astype(F32)),
    )
    cut_of_t = (spot_t // ROWS_TO) % CUTS
    for ref, value in flat:
        for c in range(CUTS):
            ref[c * rows : (c + 1) * rows, :] = jnp.where(cut_of_t == c, value, 0.0).astype(BF16)

    loads[0].wait()
    loads[3].wait()
    tiles = [(f, c, (f * CUTS + c) * LANES) for f in range(chunks) for c in range(CUTS)]
    total = jnp.zeros((rows, LANES), F32)
    for _, _, at in tiles:
        v = x[:, at : at + LANES].astype(F32)
        total += v * v
    scale = lax.rsqrt(jnp.sum(total, axis=-1, keepdims=True) / width + 1e-06)
    inv[...] = jnp.broadcast_to(scale, inv.shape)
    for f, c, at in tiles:
        v = x[:, at : at + LANES].astype(F32) * inv[...] * gain[:, at : at + LANES]
        v = v.astype(BF16)
        nrm[:, at : at + LANES] = v
        nst[c * rows : (c + 1) * rows, f * LANES : (f + 1) * LANES] = v
    fsend[...] = dot(dfwd[...], nst[...]).astype(BF16)

    pl.semaphore_wait(barrier, n_seq + 1)

    def exchange(send, recv, send_sem, recv_sem, lanes):
        mine = pl.ds(pl.multiple_of(me * PIECE, PIECE), PIECE)
        pltpu.make_async_copy(send.at[mine, lanes], recv.at[mine, lanes], recv_sem).start()

        @pl.loop(1, n_seq)
        def _(i):
            to = lax.rem(me + i, n_seq)
            theirs = pl.ds(pl.multiple_of(to * PIECE, PIECE), PIECE)
            pltpu.make_async_remote_copy(
                src_ref=send.at[theirs, lanes],
                dst_ref=recv.at[mine, lanes],
                send_sem=send_sem,
                recv_sem=recv_sem,
                device_id={"seq": to},
                device_id_type=MESH,
            ).start()

    def arrived(recv, recv_sem, lanes):
        pltpu.make_async_copy(recv.at[:, lanes], recv.at[:, lanes], recv_sem).wait()

    def sent(send, send_sem, lanes):
        part = send.at[: span - PIECE, lanes]
        pltpu.make_async_copy(part, part, send_sem).wait()

    whole = slice(0, chunks * LANES)
    exchange(fsend, frecv, fs_sem, fr_sem, whole)

    x_copy = pltpu.make_async_remote_copy(
        src_ref=x,
        dst_ref=xnext,
        send_sem=xs_sem,
        recv_sem=xr_sem,
        device_id={"pipe": before},
        device_id_type=MESH,
    )

    @pl.when(jnp.logical_not(last))
    def _():
        x_copy.start()

    loads[4].wait()
    for f in range(chunks):
        cols = slice(f * CHUNK, (f + 1) * CHUNK)
        pre = dot(nrm[...], wg[:, cols])
        s = jax.nn.sigmoid(pre)
        mf[:, cols] = pre * s
        gf[:, cols] = s * (1.0 + pre * (1.0 - s))
    loads[5].wait()

    def mixer():
        arrived(frecv, fr_sem, whole)
        mixed = dot(efwd[...], frecv[...])
        natural = dot(pick2[...], frecv[...]).astype(BF16)
        for f, c, at in tiles:
            part = (slice(c * rows, (c + 1) * rows), slice(f * LANES, (f + 1) * LANES))
            gf[:, at : at + LANES] = gf[:, at : at + LANES] * mixed[part]
            moved[:, at : at + LANES] = natural[part]

    @pl.when(jnp.logical_not(first))
    def _():
        mixer()
        x_copy.wait_recv()
        for f in range(chunks):
            cols = slice(f * CHUNK, (f + 1) * CHUNK)
            xw[:, cols] = dot(xnext[...], wo[cols, :], 1, 1)

    @pl.when(first)
    def _():
        shift[...] = jnp.zeros(shift.shape, F32)
        xw[...] = jnp.zeros(xw.shape, F32)
        xnext[...] = jnp.zeros(xnext.shape, BF16)

    for k in range(chunks):
        cot_copy(k).wait()
        deep = slice(k * CHUNK, (k + 1) * CHUNK)
        if k < chunks - 1:
            for f in range(chunks):
                cols = slice(f * CHUNK, (f + 1) * CHUNK)
                part = dot(arecv[k], wo[cols, deep], 1, 1)
                dh[:, cols] = part if k == 0 else dh[:, cols] + part
    eye = iota((rows, rows), 0) == iota((rows, rows), 1)

    c_copy = pltpu.make_async_remote_copy(
        src_ref=csend,
        dst_ref=crecv,
        send_sem=cs_sem,
        recv_sem=cr_sem,
        device_id={"pipe": before},
        device_id_type=MESH,
    )

    @pl.when(jnp.logical_not(first))
    def _():
        c_copy.wait_recv()
        spread = jnp.where(eye, jnp.broadcast_to(crecv[0:1, :], (rows, rows)), 0.0)
        shift[...] = jnp.broadcast_to(jnp.sum(spread, axis=1, keepdims=True), shift.shape)

    k = chunks - 1
    deep = slice(k * CHUNK, (k + 1) * CHUNK)
    for f in range(chunks):
        cols = slice(f * CHUNK, (f + 1) * CHUNK)
        hidden = dh[:, cols] + dot(arecv[k], wo[cols, deep], 1, 1)
        hidden = hidden - shift[:, :1] * xw[:, cols]
        dh[:, cols] = hidden
        mix = (hidden * mf[:, cols]).astype(BF16)
        dmix[:, cols] = mix
        stack = jnp.concatenate([mix[:, c * LANES : (c + 1) * LANES] for c in range(CUTS)], axis=0)
        lanes = slice(f * LANES, (f + 1) * LANES)
        bsend[:, lanes] = dot(dbwd[...], stack).astype(BF16)
        exchange(bsend, brecv, bs_sem.at[f], br_sem.at[f], lanes)

    @pl.when(first)
    def _():
        mixer()

    dgate[...] = (dh[...] * gf[...]).astype(BF16)
    for f in range(chunks):
        cols = slice(f * CHUNK, (f + 1) * CHUNK)
        gb[:, cols] = dot(dgate[...], wg[cols, :], 1, 1)
    g2_ref[...] = dot(dmix[...], moved[...], 1, 1)

    def hand(f):
        return pltpu.make_async_remote_copy(
            src_ref=asend.at[f],
            dst_ref=arecv.at[f],
            send_sem=zs_sem.at[f],
            recv_sem=zr_sem.at[f],
            device_id={"pipe": before},
            device_id_type=MESH,
        )

    total = jnp.zeros((rows, LANES), F32)
    for f in range(chunks):
        lanes = slice(f * LANES, (f + 1) * LANES)
        arrived(brecv, br_sem.at[f], lanes)
        back = dot(ebwd[...], brecv[:, lanes])
        for c in range(CUTS):
            at = f * CHUNK + c * LANES
            cols = slice(at, at + LANES)
            delta = gain[:, cols] * (back[c * rows : (c + 1) * rows, :] + gb[:, cols])
            unit = x[:, cols].astype(F32) * inv[...]
            total += delta * unit
            here = slice(c * LANES, (c + 1) * LANES)
            incoming = arecv[f, :, here].astype(F32) - shift[...] * xnext[:, cols].astype(F32)
            value = incoming + inv[...] * delta
            anat[:, cols] = value
            asend[f, :, here] = value.astype(BF16)
        if f < chunks - 1:

            @pl.when(jnp.logical_not(last))
            def _():
                hand(f).start()

    mean = jnp.sum(total, axis=-1, keepdims=True) / width
    fix = jnp.broadcast_to(mean, (rows, LANES)) * inv[...] * inv[...]
    line = jnp.sum(jnp.where(eye, fix[:, :1], 0.0), axis=0, keepdims=True)
    csend[...] = jnp.broadcast_to(line, csend.shape)

    @pl.when(jnp.logical_not(last))
    def _():
        c_copy.start()
        hand(chunks - 1).start()

    for _, _, at in tiles:
        cols = slice(at, at + LANES)
        out_ref[:, cols] = (anat[:, cols] - fix * x[:, cols].astype(F32)).astype(BF16)
    natural = dot(pick1[...], brecv[...]).astype(BF16)
    sums = jnp.zeros((rows, rows), F32)
    for c in range(CUTS):
        part = slice(c * rows, (c + 1) * rows)
        sums += dot(natural[part, :], nst[part, :], 1, 1)
    g1_ref[...] = sums

    sent(fsend, fs_sem, whole)
    for f in range(chunks):
        sent(bsend, bs_sem.at[f], slice(f * LANES, (f + 1) * LANES))

    @pl.when(jnp.logical_not(last))
    def _():
        x_copy.wait_send()
        c_copy.wait_send()
        for f in range(chunks):
            hand(f).wait_send()


def layers(n_seq, n_pipe, section_inputs, cotangent, gain, w_gate, w_out, mix_first, mix_second):
    _, rows, width = section_inputs.shape
    block = rows // 2
    chunks = width // CHUNK
    span = n_seq * PIECE
    out, g1, g2 = pl.pallas_call(
        functools.partial(kernel, n_seq, n_pipe),
        out_shape=(
            jax.ShapeDtypeStruct((rows, width), BF16),
            jax.ShapeDtypeStruct((rows, rows), F32),
            jax.ShapeDtypeStruct((rows, rows), F32),
        ),
        in_specs=[pl.BlockSpec(memory_space=pl.ANY)] * 7,
        out_specs=(pl.BlockSpec(memory_space=pltpu.VMEM),) * 3,
        scratch_shapes=[
            pltpu.VMEM((rows, width), BF16),
            pltpu.VMEM((1, width), F32),
            pltpu.VMEM((width, width), BF16),
            pltpu.VMEM((width, width), BF16),
            pltpu.VMEM((rows, block), BF16),
            pltpu.VMEM((rows, block), BF16),
            pltpu.VMEM((rows, width), BF16),
            pltpu.VMEM((rows, width), F32),
            pltpu.VMEM((rows, LANES), F32),
            pltpu.VMEM((rows, LANES), F32),
            pltpu.VMEM((rows, width), BF16),
            pltpu.VMEM((span, chunks * LANES), BF16),
            pltpu.VMEM((span, span), BF16),
            pltpu.VMEM((span, span), BF16),
            pltpu.VMEM((span, span), BF16),
            pltpu.VMEM((span, span), BF16),
            pltpu.VMEM((span, span), BF16),
            pltpu.VMEM((span, span), BF16),
            pltpu.VMEM((span, chunks * LANES), BF16),
            pltpu.VMEM((span, chunks * LANES), BF16),
            pltpu.VMEM((span, chunks * LANES), BF16),
            pltpu.VMEM((span, chunks * LANES), BF16),
            pltpu.VMEM((rows, width), BF16),
            pltpu.VMEM((rows, width), F32),
            pltpu.VMEM((rows, width), F32),
            pltpu.VMEM((rows, width), F32),
            pltpu.VMEM((rows, width), BF16),
            pltpu.VMEM((rows, width), BF16),
            pltpu.VMEM((rows, width), F32),
            pltpu.VMEM((rows, width), F32),
            pltpu.VMEM((chunks, rows, CHUNK), BF16),
            pltpu.VMEM((chunks, rows, CHUNK), BF16),
            pltpu.VMEM((8, rows), F32),
            pltpu.VMEM((8, rows), F32),
            pltpu.SemaphoreType.DMA((6,)),
            pltpu.SemaphoreType.DMA,
            pltpu.SemaphoreType.DMA,
            pltpu.SemaphoreType.DMA,
            pltpu.SemaphoreType.DMA,
            pltpu.SemaphoreType.DMA((chunks,)),
            pltpu.SemaphoreType.DMA((chunks,)),
            pltpu.SemaphoreType.DMA((chunks,)),
            pltpu.SemaphoreType.DMA((chunks,)),
            pltpu.SemaphoreType.DMA,
            pltpu.SemaphoreType.DMA,
        ],
        compiler_params=pltpu.CompilerParams(
            collective_id=0, has_side_effects=True, vmem_limit_bytes=60 * 1024 * 1024
        ),
    )(
        section_inputs[0],
        cotangent,
        gain,
        w_gate[0],
        w_out[0],
        mix_first[0].reshape(rows, block),
        mix_second[0].reshape(rows, block),
    )

    def blocks(g):
        return jnp.stack([g[:block, :block], g[block:, block:]])[None]

    return out[None], blocks(g1), blocks(g2)


def solution(mesh):
    placed = (
        P("pipe", "seq", None),
        P("seq", None),
        P("pipe", None),
        P("pipe", None, None),
        P("pipe", None, None),
        P("pipe", "seq", None, None),
        P("pipe", "seq", None, None),
    )
    return jax.shard_map(
        functools.partial(layers, mesh.shape["seq"], mesh.shape["pipe"]),
        mesh=mesh,
        in_specs=placed,
        out_specs=(
            P("pipe", "seq", None),
            P("pipe", "seq", None, None),
            P("pipe", "seq", None, None),
        ),
        check_vma=False,
    )
```

```python
import functools

import jax
import jax.numpy as jnp
from jax import lax
from jax.experimental import pallas as pl
from jax.experimental.pallas import tpu as pltpu
from jax.sharding import PartitionSpec as P

MESH = pl.DeviceIdType.MESH
F32 = jnp.float32
BF16 = jnp.bfloat16
LANES = 128
CUTS = 4
CHUNK = LANES * CUTS
ROWS_TO = 4
PIECE = ROWS_TO * CUTS


def iota(shape, axis):
    return lax.broadcasted_iota(jnp.int32, shape, axis)


def dot(a, b, da=1, db=0):
    return lax.dot_general(a, b, (((da,), (db,)), ((), ())), preferred_element_type=F32)


def as_bf16(mask):
    return jnp.where(mask, 1.0, 0.0).astype(BF16)


SCRATCH = (
    "x", "gain", "wg", "wo", "m1", "m2", "xnext", "xw", "inv", "shift",
    "nrm", "nst", "dfwd", "efwd", "dbwd", "ebwd", "pick1", "pick2", "fsend", "frecv",
    "bsend", "brecv", "moved", "mf", "gf", "dh", "dmix", "dgate", "gb", "anat",
    "abuf", "csend", "crecv", "res", "r1", "r2", "lsem", "osem", "xs_sem", "xr_sem",
    "fs_sem", "fr_sem", "bs_sem", "br_sem", "zs_sem", "zr_sem", "cs_sem", "cr_sem", "ws_sem", "wz_sem", "wxs_sem", "wxr_sem", "wys_sem", "wyr_sem", "wds_sem", "wdr_sem", "wcs_sem", "wc_sem", "ps_sem", "pr_sem", "rs_sem", "rr_sem",
)


class Refs:
    pass


def kernel(
    n_seq, n_pipe, x_hbm, cot_hbm, gain_hbm, wg_hbm, wo_hbm, m1_hbm, m2_hbm, out_hbm, g1_hbm, g2_hbm, *scratch
):
    r = Refs()
    for name, ref in zip(SCRATCH, scratch, strict=True):
        setattr(r, name, ref)
    me = lax.axis_index("seq")
    plane = lax.axis_index("pipe")
    _, rows, width = r.x.shape
    block = rows // 2
    chunks = width // CHUNK
    span = n_seq * PIECE
    whole = slice(0, chunks * LANES)
    tiles = [(f, c, (f * CUTS + c) * LANES) for f in range(chunks) for c in range(CUTS)]

    first = plane == 7
    final = plane == 0
    double = (plane == 4) | final
    supplier = (plane == 3) | (plane == 1)
    worker = jnp.logical_not(supplier)
    single = worker & jnp.logical_not(double)
    mate = jnp.where(plane >= 3, 7 - plane, 1 - plane)
    own = jnp.where(final, 1, 0)
    guest = 1 - own
    before = lax.rem(plane + n_pipe - 1, n_pipe)
    following = jnp.where(plane == 4, 2, jnp.where(plane == 2, 0, before))
    reader = jnp.where(plane == 2, 0, before)
    far = 8 if n_seq == 32 else 4
    bit_x, bit_y, bit_c = (me // far) % 2, (me // 2) % 2, me % 2
    x_mate = me + far - 2 * far * bit_x
    y_mate = me + 2 - 4 * bit_y
    core_mate = me + 1 - 2 * bit_c
    slab = width // 16

    def seq_at(device):
        return {"seq": device}

    def pipe_at(device):
        return {"pipe": device}

    def remote(src, dst, send_sem, recv_sem, device):
        return pltpu.make_async_remote_copy(
            src_ref=src,
            dst_ref=dst,
            send_sem=send_sem,
            recv_sem=recv_sem,
            device_id=device,
            device_id_type=MESH,
        )

    def landed(ref, sem):
        pltpu.make_async_copy(ref, ref, sem).wait()

    loads = [
        pltpu.make_async_copy(src, dst, r.lsem.at[i])
        for i, (src, dst) in enumerate(
            (
                (x_hbm, r.x.at[own]),
                (m1_hbm, r.m1.at[own]),
                (m2_hbm, r.m2.at[own]),
                (gain_hbm, r.gain.at[own]),
                (wg_hbm, r.wg.at[own]),
                (wo_hbm, r.wo.at[own]),
            )
        )
    ]

    @pl.when(worker)
    def _():
        for copy in loads:
            copy.start()

    def cot_copy(f):
        return pltpu.make_async_copy(
            cot_hbm.at[:, f * CHUNK : (f + 1) * CHUNK], r.abuf.at[0, f], r.zr_sem.at[f]
        )

    @pl.when(first)
    def _():
        for f in range(chunks):
            cot_copy(f).start()

    barrier = pltpu.get_barrier_semaphore()

    @pl.loop(1, n_seq)
    def _(i):
        pl.semaphore_signal(
            barrier, inc=1, device_id=seq_at(lax.rem(me + i, n_seq)), device_id_type=MESH
        )

    @pl.loop(1, n_pipe)
    def _(i):
        pl.semaphore_signal(
            barrier, inc=1, device_id=pipe_at(lax.rem(plane + i, n_pipe)), device_id_type=MESH
        )

    def exchange(send, recv, send_sem, recv_sem, lanes):
        mine = pl.ds(pl.multiple_of(me * PIECE, PIECE), PIECE)
        pltpu.make_async_copy(send.at[mine, lanes], recv.at[mine, lanes], recv_sem).start()

        @pl.loop(1, n_seq)
        def _(i):
            to = lax.rem(me + i, n_seq)
            theirs = pl.ds(pl.multiple_of(to * PIECE, PIECE), PIECE)
            remote(send.at[theirs, lanes], recv.at[mine, lanes], send_sem, recv_sem, seq_at(to)).start()

    def sent(send, send_sem, lanes):
        landed(send.at[: span - PIECE, lanes], send_sem)

    spot = iota((span, rows), 0)
    col = iota((span, rows), 1)
    dest = spot // PIECE
    quad = spot % ROWS_TO
    cut_of = (spot // ROWS_TO) % CUTS
    spot_t = iota((rows, span), 1)
    row_t = iota((rows, span), 0)
    dest_t = spot_t // PIECE
    quad_t = spot_t % ROWS_TO
    cut_of_t = (spot_t // ROWS_TO) % CUTS

    def sel1():
        return as_bf16(col == (quad % 2) * block + dest * 2 + quad // 2)

    def sel2():
        return as_bf16(col == (quad // 2) * block + dest * 2 + quad % 2)

    def sel1_t():
        return as_bf16(row_t == (quad_t % 2) * block + dest_t * 2 + quad_t // 2)

    def sel2_t():
        return as_bf16(row_t == (quad_t // 2) * block + dest_t * 2 + quad_t % 2)

    def diagonal(blocks):
        spread = as_bf16(iota((block, rows), 0) == iota((block, rows), 1) % block)
        wide = dot(blocks, spread)
        same = iota((rows, rows), 0) // block == iota((rows, rows), 1) // block
        return jnp.where(same, wide, 0.0).astype(BF16)

    def put_tall(ref, value):
        for c in range(CUTS):
            ref[:, c * rows : (c + 1) * rows] = jnp.where(cut_of == c, value, 0.0).astype(BF16)

    def put_flat(ref, value):
        for c in range(CUTS):
            ref[c * rows : (c + 1) * rows, :] = jnp.where(cut_of_t == c, value, 0.0).astype(BF16)

    def factors(at):
        d1 = diagonal(r.m1[at])
        d2 = diagonal(r.m2[at])
        put_tall(r.dfwd, dot(sel1(), d1))
        put_tall(r.dbwd.at[at], dot(sel2(), d2, 1, 1))
        put_flat(r.efwd, dot(d2, sel2_t()))
        put_flat(r.ebwd.at[at], dot(d1, sel1_t(), 0, 0))

    def norm(at):
        total = jnp.zeros((rows, LANES), F32)
        for _, _, t in tiles:
            v = r.x[at, :, t : t + LANES].astype(F32)
            total += v * v
        scale = lax.rsqrt(jnp.sum(total, axis=-1, keepdims=True) / width + 1e-06)
        scale = jnp.broadcast_to(scale, (rows, LANES))
        r.inv[at] = scale
        for f, c, t in tiles:
            v = r.x[at, :, t : t + LANES].astype(F32) * scale * r.gain[at, :, t : t + LANES]
            v = v.astype(BF16)
            r.nrm[:, t : t + LANES] = v
            r.nst[at, c * rows : (c + 1) * rows, f * LANES : (f + 1) * LANES] = v
        r.fsend[at] = dot(r.dfwd[...], r.nst[at]).astype(BF16)

    def forward(at):
        exchange(r.fsend.at[at], r.frecv.at[at], r.fs_sem.at[at], r.fr_sem.at[at], whole)

    def gate(at):
        for f in range(chunks):
            cols = slice(f * CHUNK, (f + 1) * CHUNK)
            pre = dot(r.nrm[...], r.wg[at, :, cols])
            s = jax.nn.sigmoid(pre)
            r.mf[at, :, cols] = pre * s
            r.gf[at, :, cols] = s * (1.0 + pre * (1.0 - s))

    def mixer(at):
        landed(r.frecv.at[at], r.fr_sem.at[at])
        mixed = dot(r.efwd[...], r.frecv[at])
        natural = dot(r.pick2[...], r.frecv[at]).astype(BF16)
        for f, c, t in tiles:
            part = (slice(c * rows, (c + 1) * rows), slice(f * LANES, (f + 1) * LANES))
            r.gf[at, :, t : t + LANES] = r.gf[at, :, t : t + LANES] * mixed[part]
            r.moved[at, :, t : t + LANES] = natural[part]

    @pl.when(worker)
    def _():
        loads[1].wait()
        loads[2].wait()
        put_flat(r.pick1, sel1_t().astype(F32))
        put_flat(r.pick2, sel2_t().astype(F32))
        factors(own)
        loads[0].wait()
        loads[3].wait()
        norm(own)

    pl.semaphore_wait(barrier, n_seq + n_pipe - 2)

    x_copy = remote(x_hbm, r.xnext, r.xs_sem, r.xr_sem, pipe_at(reader))
    x_sender = single | (plane == 3)
    there = jnp.where(plane == 1, 0, 1)

    def slab_at(flip_x, flip_y, j):
        unit = 4 * (1 - bit_x if flip_x else bit_x) + 2 * (1 - bit_y if flip_y else bit_y) + bit_c
        return pl.ds(pl.multiple_of((2 * unit + j) * slab, slab), slab)

    def supply():
        given = []
        for i, (src, dst) in enumerate(((wg_hbm, r.wg), (wo_hbm, r.wo))):
            for j in range(2):
                at = slab_at(0, 0, j)
                given.append(
                    remote(
                        src.at[at],
                        dst.at[there, at],
                        r.ws_sem.at[i, j],
                        r.wz_sem.at[i, j],
                        pipe_at(mate),
                    )
                )
        small = [
            remote(src, dst.at[there], r.ps_sem.at[k], r.pr_sem.at[k], pipe_at(mate))
            for k, (src, dst) in enumerate(
                ((x_hbm, r.x), (m1_hbm, r.m1), (m2_hbm, r.m2), (gain_hbm, r.gain))
            )
        ]
        return given + small[1:] + small[:1]

    @pl.when(x_sender)
    def _():
        x_copy.start()

    @pl.when(supplier)
    def _():
        for copy in supply():
            copy.start()

    def weight(i):
        return r.wo if i else r.wg

    def piece(i, j, flip_x=0, flip_y=0):
        return weight(i).at[guest, slab_at(flip_x, flip_y, j)]

    def pass_own(i, j):
        ref = piece(i, j)
        return (
            remote(ref, ref, r.wxs_sem.at[i, j], r.wxr_sem.at[i, j], seq_at(x_mate)),
            remote(ref, ref, r.wys_sem.at[i, j], r.wyr_sem.at[i, j], seq_at(y_mate)),
            remote(ref, ref, r.wcs_sem.at[0, i, j], r.wc_sem.at[i], seq_at(core_mate)),
        )

    def pass_core(i, j, flip_x, flip_y):
        ref = piece(i, j, flip_x, flip_y)
        send_sem = r.wcs_sem.at[flip_x + 2 * flip_y, i, j]
        return remote(ref, ref, send_sem, r.wc_sem.at[i], seq_at(core_mate))

    def pass_corner(i, j, flip_x, flip_y):
        ref = piece(i, j, flip_x, flip_y)
        to = y_mate if flip_x else x_mate
        return remote(ref, ref, r.wds_sem.at[i, j], r.wdr_sem.at[i, j], seq_at(to))

    def collect_own(i, j):
        landed(piece(i, j), r.wz_sem.at[i, j])
        for copy in pass_own(i, j):
            copy.start()

    def collect_sides(i, j):
        landed(piece(i, j, 1, 0), r.wxr_sem.at[i, j])

        @pl.when(bit_c == 0)
        def _():
            pass_corner(i, j, 1, 0).start()

        pass_core(i, j, 1, 0).start()
        landed(piece(i, j, 0, 1), r.wyr_sem.at[i, j])

        @pl.when(bit_c == 1)
        def _():
            pass_corner(i, j, 0, 1).start()

        pass_core(i, j, 0, 1).start()

    def collect_corner(i, j):
        landed(piece(i, j, 1, 1), r.wdr_sem.at[i, j])
        pass_core(i, j, 1, 1).start()

    def collect_rest(i):
        landed(weight(i).at[guest, : 8 * slab], r.wc_sem.at[i])

    def finish_guest():
        for j in range(2):
            collect_corner(1, j)
        collect_rest(1)
        mixer(guest)

    @pl.when(worker)
    def _():
        forward(own)
        loads[4].wait()
        gate(own)
        loads[5].wait()

    @pl.when(worker & jnp.logical_not(first))
    def _():
        mixer(own)

    def hidden_of(ref, at):
        for f in range(chunks):
            cols = slice(f * CHUNK, (f + 1) * CHUNK)
            r.xw[at, :, cols] = dot(ref[...], r.wo[at, cols, :], 1, 1)

    @pl.when(worker & jnp.logical_not(first))
    def _():
        x_copy.wait_recv()

    @pl.when(worker & jnp.logical_not(first) & jnp.logical_not(final))
    def _():
        hidden_of(r.xnext, 0)

    @pl.when(double)
    def _():
        collect_own(0, 0)
        collect_own(0, 1)
        collect_sides(0, 0)
        collect_own(1, 0)
        collect_sides(0, 1)
        collect_own(1, 1)
        collect_corner(0, 0)
        collect_corner(0, 1)
        collect_sides(1, 0)
        for k, ref in ((1, r.m1), (2, r.m2), (3, r.gain)):
            landed(ref.at[guest], r.pr_sem.at[k])
        factors(guest)
        collect_sides(1, 1)
        landed(r.x.at[guest], r.pr_sem.at[0])
        norm(guest)
        forward(guest)
        collect_rest(0)
        gate(guest)

    @pl.when(double)
    def _():
        finish_guest()
        hidden_of(r.x.at[0], 1)

    @pl.when(final)
    def _():
        hidden_of(r.xnext, 0)

    @pl.when(first)
    def _():
        r.shift[...] = jnp.zeros(r.shift.shape, F32)
        r.xw[0] = jnp.zeros((rows, width), F32)
        r.xnext[...] = jnp.zeros(r.xnext.shape, BF16)

    eye = iota((rows, rows), 0) == iota((rows, rows), 1)
    c_copy = remote(r.csend, r.crecv, r.cs_sem, r.cr_sem, pipe_at(following))

    def hand(slot, f):
        return remote(
            r.abuf.at[slot + 1, f],
            r.abuf.at[0, f],
            r.zs_sem.at[f],
            r.zr_sem.at[f],
            pipe_at(following),
        )

    def partial(slot, k):
        deep = slice(k * CHUNK, (k + 1) * CHUNK)
        for f in range(chunks):
            cols = slice(f * CHUNK, (f + 1) * CHUNK)
            part = dot(r.abuf[slot, k], r.wo[slot, cols, deep], 1, 1)
            r.dh[:, cols] = part if k == 0 else r.dh[:, cols] + part

    def results(slot):
        inv = r.inv.at[slot]
        natural = dot(r.pick1[...], r.brecv[slot]).astype(BF16)
        sums = jnp.zeros((rows, rows), F32)
        for c in range(CUTS):
            part = slice(c * rows, (c + 1) * rows)
            sums += dot(natural[part, :], r.nst[slot, part, :], 1, 1)
        for a in range(2):
            r.r1[slot, a] = sums[a * block : (a + 1) * block, a * block : (a + 1) * block]

    def outgoing(slot):
        for _, _, t in tiles:
            cols = slice(t, t + LANES)
            r.res[slot, :, cols] = (
                r.anat[:, cols] - r.shift[...] * r.x[slot, :, cols].astype(F32)
            ).astype(BF16)

    def stores(slot):
        return [
            pltpu.make_async_copy(src.at[slot], dst, r.osem.at[k])
            for k, (src, dst) in enumerate(((r.res, out_hbm), (r.r1, g1_hbm), (r.r2, g2_hbm)))
        ]

    def returns(slot, kinds=range(3)):
        pairs = ((r.res, out_hbm), (r.r1, g1_hbm), (r.r2, g2_hbm))
        return [
            remote(
                pairs[k][0].at[slot], pairs[k][1], r.rs_sem.at[k], r.rr_sem.at[k], pipe_at(mate)
            )
            for k in kinds
        ]

    def chain(slot):
        if slot == 0:
            for k in range(chunks):
                cot_copy(k).wait()
                if k < chunks - 1:
                    partial(0, k)

            @pl.when(jnp.logical_not(first))
            def _():
                c_copy.wait_recv()
                spread = jnp.where(eye, jnp.broadcast_to(r.crecv[0:1, :], (rows, rows)), 0.0)
                r.shift[...] = jnp.broadcast_to(
                    jnp.sum(spread, axis=1, keepdims=True), r.shift.shape
                )

        k = chunks - 1
        deep = slice(k * CHUNK, (k + 1) * CHUNK)
        for f in range(chunks):
            cols = slice(f * CHUNK, (f + 1) * CHUNK)
            hidden = r.dh[:, cols] + dot(r.abuf[slot, k], r.wo[slot, cols, deep], 1, 1)
            hidden = hidden - r.shift[:, :1] * r.xw[slot, :, cols]
            r.dh[:, cols] = hidden
            mix = (hidden * r.mf[slot, :, cols]).astype(BF16)
            r.dmix[:, cols] = mix
            stack = jnp.concatenate(
                [mix[:, c * LANES : (c + 1) * LANES] for c in range(CUTS)], axis=0
            )
            lanes = slice(f * LANES, (f + 1) * LANES)
            r.bsend[slot, :, lanes] = dot(r.dbwd[slot], stack).astype(BF16)
            exchange(
                r.bsend.at[slot],
                r.brecv.at[slot],
                r.bs_sem.at[slot, f],
                r.br_sem.at[slot, f],
                lanes,
            )
        if slot == 0:

            @pl.when(first)
            def _():
                mixer(0)

        r.dgate[...] = (r.dh[...] * r.gf[slot]).astype(BF16)
        for f in range(chunks):
            cols = slice(f * CHUNK, (f + 1) * CHUNK)
            r.gb[:, cols] = dot(r.dgate[...], r.wg[slot, cols, :], 1, 1)
        g2 = dot(r.dmix[...], r.moved[slot], 1, 1)
        for a in range(2):
            r.r2[slot, a] = g2[a * block : (a + 1) * block, a * block : (a + 1) * block]
        if slot == 1:
            results(0)

            @pl.when(final)
            def _():
                for copy in returns(0, (1, 2)):
                    copy.start()

        sending = single if slot == 0 else jnp.logical_not(final)
        inv = r.inv.at[slot]
        total = jnp.zeros((rows, LANES), F32)
        for f in range(chunks):
            lanes = slice(f * LANES, (f + 1) * LANES)
            landed(r.brecv.at[slot, :, lanes], r.br_sem.at[slot, f])
            back = dot(r.ebwd[slot], r.brecv[slot, :, lanes])
            for c in range(CUTS):
                t = f * CHUNK + c * LANES
                cols = slice(t, t + LANES)
                delta = r.gain[slot, :, cols] * (back[c * rows : (c + 1) * rows, :] + r.gb[:, cols])
                unit = r.x[slot, :, cols].astype(F32) * inv[...]
                total += delta * unit
                here = slice(c * LANES, (c + 1) * LANES)
                prior = r.xnext[:, cols] if slot == 0 else r.x[0, :, cols]
                incoming = r.abuf[slot, f, :, here].astype(F32) - r.shift[...] * prior.astype(F32)
                value = incoming + inv[...] * delta
                r.anat[:, cols] = value
                r.abuf[slot + 1, f, :, here] = value.astype(BF16)
            if f < chunks - 1:

                @pl.when(sending)
                def _():
                    hand(slot, f).start()

                if slot == 0:

                    @pl.when(double)
                    def _():
                        partial(1, f)

        mean = jnp.sum(total, axis=-1, keepdims=True) / width
        fix = jnp.broadcast_to(mean, (rows, LANES)) * inv[...] * inv[...]

        @pl.when(sending)
        def _():
            line = jnp.sum(jnp.where(eye, fix[:, :1], 0.0), axis=0, keepdims=True)
            r.csend[...] = jnp.broadcast_to(line, r.csend.shape)
            c_copy.start()
            hand(slot, chunks - 1).start()

        r.shift[...] = fix
        outgoing(slot)
        if slot == 0:

            @pl.when(final)
            def _():
                returns(0, (0,))[0].start()

    @pl.when(worker)
    def _():
        chain(0)

    @pl.when(single)
    def _():
        results(0)

    @pl.when(double)
    def _():
        chain(1)
        results(1)

    @pl.when(double & jnp.logical_not(final))
    def _():
        c_copy.wait_send()
        for f in range(chunks):
            hand(1, f).wait_send()
        for copy in returns(1):
            copy.start()

    @pl.when(worker)
    def _():
        for copy in stores(own):
            copy.start()
        sent(r.fsend.at[own], r.fs_sem.at[own], whole)
        for f in range(chunks):
            sent(r.bsend.at[0], r.bs_sem.at[0, f], slice(f * LANES, (f + 1) * LANES))

    @pl.when(double)
    def _():
        sent(r.fsend.at[guest], r.fs_sem.at[guest], whole)
        for f in range(chunks):
            sent(r.bsend.at[1], r.bs_sem.at[1, f], slice(f * LANES, (f + 1) * LANES))
        for i in range(2):
            for j in range(2):
                for copy in pass_own(i, j):
                    copy.wait_send()
                pass_core(i, j, 1, 0).wait_send()
                pass_core(i, j, 0, 1).wait_send()
                pass_core(i, j, 1, 1).wait_send()
                pass_corner(i, j, 1, 0).wait_send()
        for copy in returns(guest):
            copy.wait_send()

    @pl.when(x_sender)
    def _():
        x_copy.wait_send()

    @pl.when(single)
    def _():
        c_copy.wait_send()
        for f in range(chunks):
            hand(0, f).wait_send()

    @pl.when(supplier)
    def _():
        for copy in supply():
            copy.wait_send()
        for copy in returns(0):
            copy.wait_recv()

    @pl.when(worker)
    def _():
        for copy in stores(own):
            copy.wait()


def layers(n_seq, n_pipe, section_inputs, cotangent, gain, w_gate, w_out, mix_first, mix_second):
    _, rows, width = section_inputs.shape
    block = rows // 2
    chunks = width // CHUNK
    span = n_seq * PIECE
    dma = pltpu.SemaphoreType.DMA
    wide = chunks * LANES
    out, g1, g2 = pl.pallas_call(
        functools.partial(kernel, n_seq, n_pipe),
        out_shape=(
            jax.ShapeDtypeStruct((rows, width), BF16),
            jax.ShapeDtypeStruct((2, block, block), F32),
            jax.ShapeDtypeStruct((2, block, block), F32),
        ),
        in_specs=[pl.BlockSpec(memory_space=pl.ANY)] * 7,
        out_specs=(pl.BlockSpec(memory_space=pl.ANY),) * 3,
        scratch_shapes=[
            pltpu.VMEM((2, rows, width), BF16),
            pltpu.VMEM((2, 1, width), F32),
            pltpu.VMEM((2, width, width), BF16),
            pltpu.VMEM((2, width, width), BF16),
            pltpu.VMEM((2, rows, block), BF16),
            pltpu.VMEM((2, rows, block), BF16),
            pltpu.VMEM((rows, width), BF16),
            pltpu.VMEM((2, rows, width), F32),
            pltpu.VMEM((2, rows, LANES), F32),
            pltpu.VMEM((rows, LANES), F32),
            pltpu.VMEM((rows, width), BF16),
            pltpu.VMEM((2, span, wide), BF16),
            pltpu.VMEM((span, span), BF16),
            pltpu.VMEM((span, span), BF16),
            pltpu.VMEM((2, span, span), BF16),
            pltpu.VMEM((2, span, span), BF16),
            pltpu.VMEM((span, span), BF16),
            pltpu.VMEM((span, span), BF16),
            pltpu.VMEM((2, span, wide), BF16),
            pltpu.VMEM((2, span, wide), BF16),
            pltpu.VMEM((2, span, wide), BF16),
            pltpu.VMEM((2, span, wide), BF16),
            pltpu.VMEM((2, rows, width), BF16),
            pltpu.VMEM((2, rows, width), F32),
            pltpu.VMEM((2, rows, width), F32),
            pltpu.VMEM((rows, width), F32),
            pltpu.VMEM((rows, width), BF16),
            pltpu.VMEM((rows, width), BF16),
            pltpu.VMEM((rows, width), F32),
            pltpu.VMEM((rows, width), F32),
            pltpu.VMEM((3, chunks, rows, CHUNK), BF16),
            pltpu.VMEM((8, rows), F32),
            pltpu.VMEM((8, rows), F32),
            pltpu.VMEM((2, rows, width), BF16),
            pltpu.VMEM((2, 2, block, block), F32),
            pltpu.VMEM((2, 2, block, block), F32),
            dma((6,)),
            dma((3,)),
            dma,
            dma,
            dma((2,)),
            dma((2,)),
            dma((2, chunks)),
            dma((2, chunks)),
            dma((chunks,)),
            dma((chunks,)),
            dma,
            dma,
            dma((2, 2)),
            dma((2, 2)),
            dma((2, 2)),
            dma((2, 2)),
            dma((2, 2)),
            dma((2, 2)),
            dma((2, 2)),
            dma((2, 2)),
            dma((4, 2, 2)),
            dma((2,)),
            dma((4,)),
            dma((4,)),
            dma((3,)),
            dma((3,)),
        ],
        compiler_params=pltpu.CompilerParams(
            collective_id=0, has_side_effects=True, vmem_limit_bytes=60 * 1024 * 1024
        ),
    )(
        section_inputs[0],
        cotangent,
        gain,
        w_gate[0],
        w_out[0],
        mix_first[0].reshape(rows, block),
        mix_second[0].reshape(rows, block),
    )
    return out[None], g1[None], g2[None]


def solution(mesh):
    placed = (
        P("pipe", "seq", None),
        P("seq", None),
        P("pipe", None),
        P("pipe", None, None),
        P("pipe", None, None),
        P("pipe", "seq", None, None),
        P("pipe", "seq", None, None),
    )
    return jax.shard_map(
        functools.partial(layers, mesh.shape["seq"], mesh.shape["pipe"]),
        mesh=mesh,
        in_specs=placed,
        out_specs=(
            P("pipe", "seq", None),
            P("pipe", "seq", None, None),
            P("pipe", "seq", None, None),
        ),
        check_vma=False,
    )
```

```python
import functools

import jax
import jax.numpy as jnp
from jax import lax
from jax.experimental import pallas as pl
from jax.experimental.pallas import tpu as pltpu
from jax.sharding import PartitionSpec as P

MESH = pl.DeviceIdType.MESH
F32 = jnp.float32
BF16 = jnp.bfloat16
LANES = 128
CUTS = 4
CHUNK = LANES * CUTS
ROWS_TO = 4
PIECE = ROWS_TO * CUTS
PIECES = 4


def iota(shape, axis):
    return lax.broadcasted_iota(jnp.int32, shape, axis)


def dot(a, b, da=1, db=0):
    return lax.dot_general(a, b, (((da,), (db,)), ((), ())), preferred_element_type=F32)


def as_bf16(mask):
    return jnp.where(mask, 1.0, 0.0).astype(BF16)


SCRATCH = (
    "x", "gain", "wg", "wo", "m1", "m2", "xnext", "xw", "inv", "shift",
    "nrm", "nst", "dfwd", "efwd", "dbwd", "ebwd", "pick1", "pick2", "fsend", "frecv",
    "bsend", "brecv", "moved", "mf", "gf", "dh", "dmix", "dgate", "gb", "anat",
    "abuf", "csend", "crecv", "res", "r1", "r2", "lsem", "osem", "xs_sem", "xr_sem",
    "fs_sem", "fr_sem", "bs_sem", "br_sem", "zs_sem", "zr_sem", "cs_sem", "cr_sem", "ws_sem", "wz_sem", "wxs_sem", "wxr_sem", "wys_sem", "wyr_sem", "wds_sem", "wdr_sem", "wcs_sem", "wc_sem", "ps_sem", "pr_sem", "rs_sem", "rr_sem",
)


class Refs:
    pass


def kernel(
    n_seq, n_pipe, x_hbm, cot_hbm, gain_hbm, wg_hbm, wo_hbm, m1_hbm, m2_hbm, out_hbm, g1_hbm, g2_hbm, *scratch
):
    r = Refs()
    for name, ref in zip(SCRATCH, scratch, strict=True):
        setattr(r, name, ref)
    me = lax.axis_index("seq")
    plane = lax.axis_index("pipe")
    _, rows, width = r.x.shape
    block = rows // 2
    chunks = width // CHUNK
    span = n_seq * PIECE
    whole = slice(0, chunks * LANES)
    tiles = [(f, c, (f * CUTS + c) * LANES) for f in range(chunks) for c in range(CUTS)]

    first = plane == 7
    final = plane == 0
    double = (plane == 4) | final
    supplier = (plane == 3) | (plane == 1)
    worker = jnp.logical_not(supplier)
    single = worker & jnp.logical_not(double)
    mate = jnp.where(plane >= 3, 7 - plane, 1 - plane)
    own = jnp.where(final, 1, 0)
    guest = 1 - own
    before = lax.rem(plane + n_pipe - 1, n_pipe)
    following = jnp.where(plane == 4, 2, jnp.where(plane == 2, 0, before))
    reader = jnp.where(plane == 2, 0, before)
    far = 8 if n_seq == 32 else 4
    bit_x, bit_y, bit_c = (me // far) % 2, (me // 2) % 2, me % 2
    n_x, n_y = n_seq // far, far // 2
    at_x, at_y = me // far, (me // 2) % n_y

    def across(place, bit, count, j):
        step = 1 - 2 * bit if j % 2 == 0 else 2 * bit - 1
        return lax.rem(place + step + count, count)

    def x_mate(j):
        return me + far * (across(at_x, bit_x, n_x, j) - at_x)

    def y_mate(j):
        return me + 2 * (across(at_y, bit_y, n_y, j) - at_y)

    core_mate = me + 1 - 2 * bit_c
    slab = width // (8 * PIECES)

    def seq_at(device):
        return {"seq": device}

    def pipe_at(device):
        return {"pipe": device}

    def remote(src, dst, send_sem, recv_sem, device):
        return pltpu.make_async_remote_copy(
            src_ref=src,
            dst_ref=dst,
            send_sem=send_sem,
            recv_sem=recv_sem,
            device_id=device,
            device_id_type=MESH,
        )

    def landed(ref, sem):
        pltpu.make_async_copy(ref, ref, sem).wait()

    loads = [
        pltpu.make_async_copy(src, dst, r.lsem.at[i])
        for i, (src, dst) in enumerate(
            (
                (x_hbm, r.x.at[own]),
                (m1_hbm, r.m1.at[own]),
                (m2_hbm, r.m2.at[own]),
                (gain_hbm, r.gain.at[own]),
                (wg_hbm, r.wg.at[own]),
                (wo_hbm, r.wo.at[own]),
            )
        )
    ]

    @pl.when(worker)
    def _():
        for copy in loads:
            copy.start()

    def cot_copy(f):
        return pltpu.make_async_copy(
            cot_hbm.at[:, f * CHUNK : (f + 1) * CHUNK], r.abuf.at[0, f], r.zr_sem.at[f]
        )

    @pl.when(first)
    def _():
        for f in range(chunks):
            cot_copy(f).start()

    barrier = pltpu.get_barrier_semaphore()

    @pl.loop(1, n_seq)
    def _(i):
        pl.semaphore_signal(
            barrier, inc=1, device_id=seq_at(lax.rem(me + i, n_seq)), device_id_type=MESH
        )

    @pl.loop(1, n_pipe)
    def _(i):
        pl.semaphore_signal(
            barrier, inc=1, device_id=pipe_at(lax.rem(plane + i, n_pipe)), device_id_type=MESH
        )

    def exchange(send, recv, send_sem, recv_sem, lanes):
        mine = pl.ds(pl.multiple_of(me * PIECE, PIECE), PIECE)
        pltpu.make_async_copy(send.at[mine, lanes], recv.at[mine, lanes], recv_sem).start()

        @pl.loop(1, n_seq)
        def _(i):
            to = lax.rem(me + i, n_seq)
            theirs = pl.ds(pl.multiple_of(to * PIECE, PIECE), PIECE)
            remote(send.at[theirs, lanes], recv.at[mine, lanes], send_sem, recv_sem, seq_at(to)).start()

    def sent(send, send_sem, lanes):
        landed(send.at[: span - PIECE, lanes], send_sem)

    spot = iota((span, rows), 0)
    col = iota((span, rows), 1)
    dest = spot // PIECE
    quad = spot % ROWS_TO
    cut_of = (spot // ROWS_TO) % CUTS
    spot_t = iota((rows, span), 1)
    row_t = iota((rows, span), 0)
    dest_t = spot_t // PIECE
    quad_t = spot_t % ROWS_TO
    cut_of_t = (spot_t // ROWS_TO) % CUTS

    def sel1():
        return as_bf16(col == (quad % 2) * block + dest * 2 + quad // 2)

    def sel2():
        return as_bf16(col == (quad // 2) * block + dest * 2 + quad % 2)

    def sel1_t():
        return as_bf16(row_t == (quad_t % 2) * block + dest_t * 2 + quad_t // 2)

    def sel2_t():
        return as_bf16(row_t == (quad_t // 2) * block + dest_t * 2 + quad_t % 2)

    def diagonal(blocks):
        spread = as_bf16(iota((block, rows), 0) == iota((block, rows), 1) % block)
        wide = dot(blocks, spread)
        same = iota((rows, rows), 0) // block == iota((rows, rows), 1) // block
        return jnp.where(same, wide, 0.0).astype(BF16)

    def put_tall(ref, value):
        for c in range(CUTS):
            ref[:, c * rows : (c + 1) * rows] = jnp.where(cut_of == c, value, 0.0).astype(BF16)

    def put_flat(ref, value):
        for c in range(CUTS):
            ref[c * rows : (c + 1) * rows, :] = jnp.where(cut_of_t == c, value, 0.0).astype(BF16)

    def factors(at):
        d1 = diagonal(r.m1[at])
        d2 = diagonal(r.m2[at])
        put_tall(r.dfwd, dot(sel1(), d1))
        put_tall(r.dbwd.at[at], dot(sel2(), d2, 1, 1))
        put_flat(r.efwd, dot(d2, sel2_t()))
        put_flat(r.ebwd.at[at], dot(d1, sel1_t(), 0, 0))

    def norm(at):
        total = jnp.zeros((rows, LANES), F32)
        for _, _, t in tiles:
            v = r.x[at, :, t : t + LANES].astype(F32)
            total += v * v
        scale = lax.rsqrt(jnp.sum(total, axis=-1, keepdims=True) / width + 1e-06)
        scale = jnp.broadcast_to(scale, (rows, LANES))
        r.inv[at] = scale
        for f, c, t in tiles:
            v = r.x[at, :, t : t + LANES].astype(F32) * scale * r.gain[at, :, t : t + LANES]
            v = v.astype(BF16)
            r.nrm[:, t : t + LANES] = v
            r.nst[at, c * rows : (c + 1) * rows, f * LANES : (f + 1) * LANES] = v
        r.fsend[at] = dot(r.dfwd[...], r.nst[at]).astype(BF16)

    def forward(at):
        exchange(r.fsend.at[at], r.frecv.at[at], r.fs_sem.at[at], r.fr_sem.at[at], whole)

    def gate(at):
        for f in range(chunks):
            cols = slice(f * CHUNK, (f + 1) * CHUNK)
            pre = dot(r.nrm[...], r.wg[at, :, cols])
            s = jax.nn.sigmoid(pre)
            r.mf[at, :, cols] = pre * s
            r.gf[at, :, cols] = s * (1.0 + pre * (1.0 - s))

    def mixer(at):
        landed(r.frecv.at[at], r.fr_sem.at[at])
        mixed = dot(r.efwd[...], r.frecv[at])
        natural = dot(r.pick2[...], r.frecv[at]).astype(BF16)
        for f, c, t in tiles:
            part = (slice(c * rows, (c + 1) * rows), slice(f * LANES, (f + 1) * LANES))
            r.gf[at, :, t : t + LANES] = r.gf[at, :, t : t + LANES] * mixed[part]
            r.moved[at, :, t : t + LANES] = natural[part]

    @pl.when(worker)
    def _():
        loads[1].wait()
        loads[2].wait()
        put_flat(r.pick1, sel1_t().astype(F32))
        put_flat(r.pick2, sel2_t().astype(F32))
        factors(own)
        loads[0].wait()
        loads[3].wait()
        norm(own)

    pl.semaphore_wait(barrier, n_seq + n_pipe - 2)

    x_copy = remote(x_hbm, r.xnext, r.xs_sem, r.xr_sem, pipe_at(reader))
    x_sender = single | (plane == 3)
    there = jnp.where(plane == 1, 0, 1)

    def slab_at(flip_x, flip_y, j):
        unit = 4 * (1 - bit_x if flip_x else bit_x) + 2 * (1 - bit_y if flip_y else bit_y) + bit_c
        return pl.ds(pl.multiple_of((PIECES * unit + j) * slab, slab), slab)

    def supply():
        given = []
        for i, (src, dst) in enumerate(((wg_hbm, r.wg), (wo_hbm, r.wo))):
            for j in range(PIECES):
                at = slab_at(0, 0, j)
                given.append(
                    remote(
                        src.at[at],
                        dst.at[there, at],
                        r.ws_sem.at[i, j],
                        r.wz_sem.at[i, j],
                        pipe_at(mate),
                    )
                )
        small = [
            remote(src, dst.at[there], r.ps_sem.at[k], r.pr_sem.at[k], pipe_at(mate))
            for k, (src, dst) in enumerate(
                ((x_hbm, r.x), (m1_hbm, r.m1), (m2_hbm, r.m2), (gain_hbm, r.gain))
            )
        ]
        return small + given

    @pl.when(x_sender)
    def _():
        x_copy.start()

    @pl.when(supplier)
    def _():
        for copy in supply():
            copy.start()

    def weight(i):
        return r.wo if i else r.wg

    def piece(i, j, flip_x=0, flip_y=0):
        return weight(i).at[guest, slab_at(flip_x, flip_y, j)]

    def pass_own(i, j):
        ref = piece(i, j)
        return (
            remote(ref, ref, r.wxs_sem.at[i, j], r.wxr_sem.at[i, j], seq_at(x_mate(j))),
            remote(ref, ref, r.wys_sem.at[i, j], r.wyr_sem.at[i, j], seq_at(y_mate(j))),
            remote(ref, ref, r.wcs_sem.at[0, i, j], r.wc_sem.at[i], seq_at(core_mate)),
        )

    def pass_core(i, j, flip_x, flip_y):
        ref = piece(i, j, flip_x, flip_y)
        send_sem = r.wcs_sem.at[flip_x + 2 * flip_y, i, j]
        return remote(ref, ref, send_sem, r.wc_sem.at[i], seq_at(core_mate))

    def pass_corner(i, j, flip_x, flip_y):
        ref = piece(i, j, flip_x, flip_y)
        to = y_mate(j) if flip_x else x_mate(j)
        return remote(ref, ref, r.wds_sem.at[i, j], r.wdr_sem.at[i, j], seq_at(to))

    def collect_own(i, j):
        landed(piece(i, j), r.wz_sem.at[i, j])
        for copy in pass_own(i, j):
            copy.start()

    def collect_sides(i, j):
        landed(piece(i, j, 1, 0), r.wxr_sem.at[i, j])

        @pl.when(bit_c == 0)
        def _():
            pass_corner(i, j, 1, 0).start()

        pass_core(i, j, 1, 0).start()
        landed(piece(i, j, 0, 1), r.wyr_sem.at[i, j])

        @pl.when(bit_c == 1)
        def _():
            pass_corner(i, j, 0, 1).start()

        pass_core(i, j, 0, 1).start()

    def collect_corner(i, j):
        landed(piece(i, j, 1, 1), r.wdr_sem.at[i, j])
        pass_core(i, j, 1, 1).start()

    def collect_rest(i):
        landed(weight(i).at[guest, : width // 2], r.wc_sem.at[i])

    def finish_guest():
        for j in (PIECES - 2, PIECES - 1):
            collect_corner(1, j)
        collect_rest(1)

    @pl.when(worker)
    def _():
        forward(own)
        loads[4].wait()
        gate(own)
        loads[5].wait()

    @pl.when(worker & jnp.logical_not(first))
    def _():
        mixer(own)

    def hidden_of(ref, at):
        for f in range(chunks):
            cols = slice(f * CHUNK, (f + 1) * CHUNK)
            r.xw[at, :, cols] = dot(ref[...], r.wo[at, cols, :], 1, 1)

    @pl.when(worker & jnp.logical_not(first))
    def _():
        x_copy.wait_recv()

    @pl.when(worker & jnp.logical_not(first) & jnp.logical_not(final))
    def _():
        hidden_of(r.xnext, 0)

    @pl.when(double)
    def _():
        for k, ref in enumerate((r.x, r.m1, r.m2, r.gain)):
            landed(ref.at[guest], r.pr_sem.at[k])
        factors(guest)
        norm(guest)
        forward(guest)
        steps = [(i, j) for i in range(2) for j in range(PIECES)]
        for t in range(len(steps) + 2):
            if t < len(steps):
                collect_own(*steps[t])
            if t >= 2:
                collect_sides(*steps[t - 2])
            if 3 <= t < len(steps) + 1:
                collect_corner(*steps[t - 3])
            if t == PIECES + 2:
                collect_rest(0)
                gate(guest)
                mixer(guest)

    @pl.when(double)
    def _():
        finish_guest()
        hidden_of(r.x.at[0], 1)

    @pl.when(final)
    def _():
        hidden_of(r.xnext, 0)

    @pl.when(first)
    def _():
        r.shift[...] = jnp.zeros(r.shift.shape, F32)
        r.xw[0] = jnp.zeros((rows, width), F32)
        r.xnext[...] = jnp.zeros(r.xnext.shape, BF16)

    eye = iota((rows, rows), 0) == iota((rows, rows), 1)
    c_copy = remote(r.csend, r.crecv, r.cs_sem, r.cr_sem, pipe_at(following))

    def hand(slot, f):
        return remote(
            r.abuf.at[slot + 1, f],
            r.abuf.at[0, f],
            r.zs_sem.at[f],
            r.zr_sem.at[f],
            pipe_at(following),
        )

    def partial(slot, k):
        deep = slice(k * CHUNK, (k + 1) * CHUNK)
        for f in range(chunks):
            cols = slice(f * CHUNK, (f + 1) * CHUNK)
            part = dot(r.abuf[slot, k], r.wo[slot, cols, deep], 1, 1)
            r.dh[:, cols] = part if k == 0 else r.dh[:, cols] + part

    def results(slot):
        inv = r.inv.at[slot]
        natural = dot(r.pick1[...], r.brecv[slot]).astype(BF16)
        sums = jnp.zeros((rows, rows), F32)
        for c in range(CUTS):
            part = slice(c * rows, (c + 1) * rows)
            sums += dot(natural[part, :], r.nst[slot, part, :], 1, 1)
        for a in range(2):
            r.r1[slot, a] = sums[a * block : (a + 1) * block, a * block : (a + 1) * block]

    def outgoing(slot):
        for _, _, t in tiles:
            cols = slice(t, t + LANES)
            r.res[slot, :, cols] = (
                r.anat[:, cols] - r.shift[...] * r.x[slot, :, cols].astype(F32)
            ).astype(BF16)

    def stores(slot):
        return [
            pltpu.make_async_copy(src.at[slot], dst, r.osem.at[k])
            for k, (src, dst) in enumerate(((r.res, out_hbm), (r.r1, g1_hbm), (r.r2, g2_hbm)))
        ]

    def returns(slot, kinds=range(3)):
        pairs = ((r.res, out_hbm), (r.r1, g1_hbm), (r.r2, g2_hbm))
        return [
            remote(
                pairs[k][0].at[slot], pairs[k][1], r.rs_sem.at[k], r.rr_sem.at[k], pipe_at(mate)
            )
            for k in kinds
        ]

    def chain(slot):
        if slot == 0:
            for k in range(chunks):
                cot_copy(k).wait()
                if k < chunks - 1:
                    partial(0, k)

            @pl.when(jnp.logical_not(first))
            def _():
                c_copy.wait_recv()
                spread = jnp.where(eye, jnp.broadcast_to(r.crecv[0:1, :], (rows, rows)), 0.0)
                r.shift[...] = jnp.broadcast_to(
                    jnp.sum(spread, axis=1, keepdims=True), r.shift.shape
                )

        k = chunks - 1
        deep = slice(k * CHUNK, (k + 1) * CHUNK)
        for f in range(chunks):
            cols = slice(f * CHUNK, (f + 1) * CHUNK)
            hidden = r.dh[:, cols] + dot(r.abuf[slot, k], r.wo[slot, cols, deep], 1, 1)
            hidden = hidden - r.shift[:, :1] * r.xw[slot, :, cols]
            r.dh[:, cols] = hidden
            mix = (hidden * r.mf[slot, :, cols]).astype(BF16)
            r.dmix[:, cols] = mix
            stack = jnp.concatenate(
                [mix[:, c * LANES : (c + 1) * LANES] for c in range(CUTS)], axis=0
            )
            lanes = slice(f * LANES, (f + 1) * LANES)
            r.bsend[slot, :, lanes] = dot(r.dbwd[slot], stack).astype(BF16)
            exchange(
                r.bsend.at[slot],
                r.brecv.at[slot],
                r.bs_sem.at[slot, f],
                r.br_sem.at[slot, f],
                lanes,
            )
        if slot == 0:

            @pl.when(first)
            def _():
                mixer(0)

        r.dgate[...] = (r.dh[...] * r.gf[slot]).astype(BF16)
        for f in range(chunks):
            cols = slice(f * CHUNK, (f + 1) * CHUNK)
            r.gb[:, cols] = dot(r.dgate[...], r.wg[slot, cols, :], 1, 1)
        g2 = dot(r.dmix[...], r.moved[slot], 1, 1)
        for a in range(2):
            r.r2[slot, a] = g2[a * block : (a + 1) * block, a * block : (a + 1) * block]
        if slot == 1:
            results(0)

            @pl.when(final)
            def _():
                for copy in returns(0, (1, 2)):
                    copy.start()

        sending = single if slot == 0 else jnp.logical_not(final)
        inv = r.inv.at[slot]
        total = jnp.zeros((rows, LANES), F32)
        for f in range(chunks):
            lanes = slice(f * LANES, (f + 1) * LANES)
            landed(r.brecv.at[slot, :, lanes], r.br_sem.at[slot, f])
            back = dot(r.ebwd[slot], r.brecv[slot, :, lanes])
            for c in range(CUTS):
                t = f * CHUNK + c * LANES
                cols = slice(t, t + LANES)
                delta = r.gain[slot, :, cols] * (back[c * rows : (c + 1) * rows, :] + r.gb[:, cols])
                unit = r.x[slot, :, cols].astype(F32) * inv[...]
                total += delta * unit
                here = slice(c * LANES, (c + 1) * LANES)
                prior = r.xnext[:, cols] if slot == 0 else r.x[0, :, cols]
                incoming = r.abuf[slot, f, :, here].astype(F32) - r.shift[...] * prior.astype(F32)
                value = incoming + inv[...] * delta
                r.anat[:, cols] = value
                r.abuf[slot + 1, f, :, here] = value.astype(BF16)
            if f < chunks - 1:

                @pl.when(sending)
                def _():
                    hand(slot, f).start()

                if slot == 0:

                    @pl.when(double)
                    def _():
                        partial(1, f)

        mean = jnp.sum(total, axis=-1, keepdims=True) / width
        fix = jnp.broadcast_to(mean, (rows, LANES)) * inv[...] * inv[...]

        @pl.when(sending)
        def _():
            line = jnp.sum(jnp.where(eye, fix[:, :1], 0.0), axis=0, keepdims=True)
            r.csend[...] = jnp.broadcast_to(line, r.csend.shape)
            c_copy.start()
            hand(slot, chunks - 1).start()

        r.shift[...] = fix
        outgoing(slot)
        if slot == 0:

            @pl.when(final)
            def _():
                returns(0, (0,))[0].start()

    @pl.when(worker)
    def _():
        chain(0)

    @pl.when(single)
    def _():
        results(0)

    @pl.when(double)
    def _():
        chain(1)
        results(1)

    @pl.when(double & jnp.logical_not(final))
    def _():
        c_copy.wait_send()
        for f in range(chunks):
            hand(1, f).wait_send()
        for copy in returns(1):
            copy.start()

    @pl.when(worker)
    def _():
        for copy in stores(own):
            copy.start()
        sent(r.fsend.at[own], r.fs_sem.at[own], whole)
        for f in range(chunks):
            sent(r.bsend.at[0], r.bs_sem.at[0, f], slice(f * LANES, (f + 1) * LANES))

    @pl.when(double)
    def _():
        sent(r.fsend.at[guest], r.fs_sem.at[guest], whole)
        for f in range(chunks):
            sent(r.bsend.at[1], r.bs_sem.at[1, f], slice(f * LANES, (f + 1) * LANES))
        for i in range(2):
            for j in range(PIECES):
                for copy in pass_own(i, j):
                    copy.wait_send()
                pass_core(i, j, 1, 0).wait_send()
                pass_core(i, j, 0, 1).wait_send()
                pass_core(i, j, 1, 1).wait_send()
                pass_corner(i, j, 1, 0).wait_send()
        for copy in returns(guest):
            copy.wait_send()

    @pl.when(x_sender)
    def _():
        x_copy.wait_send()

    @pl.when(single)
    def _():
        c_copy.wait_send()
        for f in range(chunks):
            hand(0, f).wait_send()

    @pl.when(supplier)
    def _():
        for copy in supply():
            copy.wait_send()
        for copy in returns(0):
            copy.wait_recv()

    @pl.when(worker)
    def _():
        for copy in stores(own):
            copy.wait()


def layers(n_seq, n_pipe, section_inputs, cotangent, gain, w_gate, w_out, mix_first, mix_second):
    _, rows, width = section_inputs.shape
    block = rows // 2
    chunks = width // CHUNK
    span = n_seq * PIECE
    dma = pltpu.SemaphoreType.DMA
    wide = chunks * LANES
    out, g1, g2 = pl.pallas_call(
        functools.partial(kernel, n_seq, n_pipe),
        out_shape=(
            jax.ShapeDtypeStruct((rows, width), BF16),
            jax.ShapeDtypeStruct((2, block, block), F32),
            jax.ShapeDtypeStruct((2, block, block), F32),
        ),
        in_specs=[pl.BlockSpec(memory_space=pl.ANY)] * 7,
        out_specs=(pl.BlockSpec(memory_space=pl.ANY),) * 3,
        scratch_shapes=[
            pltpu.VMEM((2, rows, width), BF16),
            pltpu.VMEM((2, 1, width), F32),
            pltpu.VMEM((2, width, width), BF16),
            pltpu.VMEM((2, width, width), BF16),
            pltpu.VMEM((2, rows, block), BF16),
            pltpu.VMEM((2, rows, block), BF16),
            pltpu.VMEM((rows, width), BF16),
            pltpu.VMEM((2, rows, width), F32),
            pltpu.VMEM((2, rows, LANES), F32),
            pltpu.VMEM((rows, LANES), F32),
            pltpu.VMEM((rows, width), BF16),
            pltpu.VMEM((2, span, wide), BF16),
            pltpu.VMEM((span, span), BF16),
            pltpu.VMEM((span, span), BF16),
            pltpu.VMEM((2, span, span), BF16),
            pltpu.VMEM((2, span, span), BF16),
            pltpu.VMEM((span, span), BF16),
            pltpu.VMEM((span, span), BF16),
            pltpu.VMEM((2, span, wide), BF16),
            pltpu.VMEM((2, span, wide), BF16),
            pltpu.VMEM((2, span, wide), BF16),
            pltpu.VMEM((2, span, wide), BF16),
            pltpu.VMEM((2, rows, width), BF16),
            pltpu.VMEM((2, rows, width), F32),
            pltpu.VMEM((2, rows, width), F32),
            pltpu.VMEM((rows, width), F32),
            pltpu.VMEM((rows, width), BF16),
            pltpu.VMEM((rows, width), BF16),
            pltpu.VMEM((rows, width), F32),
            pltpu.VMEM((rows, width), F32),
            pltpu.VMEM((3, chunks, rows, CHUNK), BF16),
            pltpu.VMEM((8, rows), F32),
            pltpu.VMEM((8, rows), F32),
            pltpu.VMEM((2, rows, width), BF16),
            pltpu.VMEM((2, 2, block, block), F32),
            pltpu.VMEM((2, 2, block, block), F32),
            dma((6,)),
            dma((3,)),
            dma,
            dma,
            dma((2,)),
            dma((2,)),
            dma((2, chunks)),
            dma((2, chunks)),
            dma((chunks,)),
            dma((chunks,)),
            dma,
            dma,
            dma((2, PIECES)),
            dma((2, PIECES)),
            dma((2, PIECES)),
            dma((2, PIECES)),
            dma((2, PIECES)),
            dma((2, PIECES)),
            dma((2, PIECES)),
            dma((2, PIECES)),
            dma((4, 2, PIECES)),
            dma((2,)),
            dma((4,)),
            dma((4,)),
            dma((3,)),
            dma((3,)),
        ],
        compiler_params=pltpu.CompilerParams(
            collective_id=0, has_side_effects=True, vmem_limit_bytes=60 * 1024 * 1024
        ),
    )(
        section_inputs[0],
        cotangent,
        gain,
        w_gate[0],
        w_out[0],
        mix_first[0].reshape(rows, block),
        mix_second[0].reshape(rows, block),
    )
    return out[None], g1[None], g2[None]


def solution(mesh):
    placed = (
        P("pipe", "seq", None),
        P("seq", None),
        P("pipe", None),
        P("pipe", None, None),
        P("pipe", None, None),
        P("pipe", "seq", None, None),
        P("pipe", "seq", None, None),
    )
    return jax.shard_map(
        functools.partial(layers, mesh.shape["seq"], mesh.shape["pipe"]),
        mesh=mesh,
        in_specs=placed,
        out_specs=(
            P("pipe", "seq", None),
            P("pipe", "seq", None, None),
            P("pipe", "seq", None, None),
        ),
        check_vma=False,
    )
```

```python
import functools

import jax
import jax.numpy as jnp
from jax import lax
from jax.experimental import pallas as pl
from jax.experimental.pallas import tpu as pltpu
from jax.sharding import PartitionSpec as P

MESH = pl.DeviceIdType.MESH
F32 = jnp.float32
BF16 = jnp.bfloat16
LANES = 128
CUTS = 4
CHUNK = LANES * CUTS
ROWS_TO = 4
PIECE = ROWS_TO * CUTS
PIECES = 4


def iota(shape, axis):
    return lax.broadcasted_iota(jnp.int32, shape, axis)


def dot(a, b, da=1, db=0):
    return lax.dot_general(a, b, (((da,), (db,)), ((), ())), preferred_element_type=F32)


def as_bf16(mask):
    return jnp.where(mask, 1.0, 0.0).astype(BF16)


SCRATCH = (
    "x", "gain", "wg", "wo", "m1", "m2", "xnext", "xw", "inv", "shift",
    "nrm", "nst", "dfwd", "efwd", "dbwd", "ebwd", "pick1", "pick2", "fsend", "frecv",
    "bsend", "brecv", "moved", "mf", "gf", "dh", "dmix", "dgate", "gb", "anat",
    "abuf", "csend", "crecv", "res", "r1", "r2", "lsem", "osem", "xs_sem", "xr_sem",
    "fs_sem", "fr_sem", "bs_sem", "br_sem", "zs_sem", "zr_sem", "cs_sem", "cr_sem", "ws_sem", "wz_sem", "wxs_sem", "wxr_sem", "wys_sem", "wyr_sem", "wds_sem", "wdr_sem", "wcs_sem", "wc_sem", "ps_sem", "pr_sem", "rs_sem", "rr_sem",
)


class Refs:
    pass


def kernel(
    n_seq, n_pipe, x_hbm, cot_hbm, gain_hbm, wg_hbm, wo_hbm, m1_hbm, m2_hbm, out_hbm, g1_hbm, g2_hbm, *scratch
):
    r = Refs()
    for name, ref in zip(SCRATCH, scratch, strict=True):
        setattr(r, name, ref)
    me = lax.axis_index("seq")
    plane = lax.axis_index("pipe")
    _, rows, width = r.x.shape
    block = rows // 2
    chunks = width // CHUNK
    span = n_seq * PIECE
    whole = slice(0, chunks * LANES)
    tiles = [(f, c, (f * CUTS + c) * LANES) for f in range(chunks) for c in range(CUTS)]

    first = plane == 7
    final = plane == 0
    double = (plane == 4) | final
    supplier = (plane == 3) | (plane == 1)
    worker = jnp.logical_not(supplier)
    single = worker & jnp.logical_not(double)
    mate = jnp.where(plane >= 3, 7 - plane, 1 - plane)
    own = jnp.where(final, 1, 0)
    guest = 1 - own
    before = lax.rem(plane + n_pipe - 1, n_pipe)
    following = jnp.where(plane == 4, 2, jnp.where(plane == 2, 0, before))
    reader = jnp.where(plane == 2, 0, before)
    far = 8 if n_seq == 32 else 4
    bit_x, bit_y, bit_c = (me // far) % 2, (me // 2) % 2, me % 2
    n_x, n_y = n_seq // far, far // 2
    at_x, at_y = me // far, (me // 2) % n_y

    def across(place, bit, count, j):
        step = 1 - 2 * bit if j % 2 == 0 else 2 * bit - 1
        return lax.rem(place + step + count, count)

    def x_mate(j):
        return me + far * (across(at_x, bit_x, n_x, j) - at_x)

    def y_mate(j):
        return me + 2 * (across(at_y, bit_y, n_y, j) - at_y)

    core_mate = me + 1 - 2 * bit_c
    slab = width // (8 * PIECES)

    def seq_at(device):
        return {"seq": device}

    def pipe_at(device):
        return {"pipe": device}

    def remote(src, dst, send_sem, recv_sem, device):
        return pltpu.make_async_remote_copy(
            src_ref=src,
            dst_ref=dst,
            send_sem=send_sem,
            recv_sem=recv_sem,
            device_id=device,
            device_id_type=MESH,
        )

    def landed(ref, sem):
        pltpu.make_async_copy(ref, ref, sem).wait()

    loads = [
        pltpu.make_async_copy(src, dst, r.lsem.at[i])
        for i, (src, dst) in enumerate(
            (
                (x_hbm, r.x.at[own]),
                (m1_hbm, r.m1.at[own]),
                (m2_hbm, r.m2.at[own]),
                (gain_hbm, r.gain.at[own]),
                (wg_hbm, r.wg.at[own]),
                (wo_hbm, r.wo.at[own]),
            )
        )
    ]

    @pl.when(worker)
    def _():
        for copy in loads:
            copy.start()

    def cot_copy(f):
        return pltpu.make_async_copy(
            cot_hbm.at[:, f * CHUNK : (f + 1) * CHUNK], r.abuf.at[0, f], r.zr_sem.at[f]
        )

    @pl.when(first)
    def _():
        for f in range(chunks):
            cot_copy(f).start()

    barrier = pltpu.get_barrier_semaphore()

    @pl.loop(1, n_seq)
    def _(i):
        pl.semaphore_signal(
            barrier, inc=1, device_id=seq_at(lax.rem(me + i, n_seq)), device_id_type=MESH
        )

    @pl.loop(1, n_pipe)
    def _(i):
        pl.semaphore_signal(
            barrier, inc=1, device_id=pipe_at(lax.rem(plane + i, n_pipe)), device_id_type=MESH
        )

    places_x = [lax.rem(at_x + d, n_x) for d in range(n_x)]
    places_y = [lax.rem(at_y + d, n_y) for d in range(n_y)]
    places_c = [bit_c, 1 - bit_c]
    others = sorted(
        ((dx, dy, dc) for dx in range(n_x) for dy in range(n_y) for dc in range(2) if dx or dy or dc),
        key=lambda d: -3 * (min(d[0], n_x - d[0]) + min(d[1], n_y - d[1])) - d[2],
    )

    def exchange(send, recv, send_sem, recv_sem, lanes):
        mine = pl.ds(pl.multiple_of(me * PIECE, PIECE), PIECE)
        pltpu.make_async_copy(send.at[mine, lanes], recv.at[mine, lanes], recv_sem).start()

        for dx, dy, dc in others:
            to = far * places_x[dx] + 2 * places_y[dy] + places_c[dc]
            theirs = pl.ds(pl.multiple_of(to * PIECE, PIECE), PIECE)
            remote(send.at[theirs, lanes], recv.at[mine, lanes], send_sem, recv_sem, seq_at(to)).start()

    def sent(send, send_sem, lanes):
        landed(send.at[: span - PIECE, lanes], send_sem)

    spot = iota((span, rows), 0)
    col = iota((span, rows), 1)
    dest = spot // PIECE
    quad = spot % ROWS_TO
    cut_of = (spot // ROWS_TO) % CUTS
    spot_t = iota((rows, span), 1)
    row_t = iota((rows, span), 0)
    dest_t = spot_t // PIECE
    quad_t = spot_t % ROWS_TO
    cut_of_t = (spot_t // ROWS_TO) % CUTS

    def sel1():
        return as_bf16(col == (quad % 2) * block + dest * 2 + quad // 2)

    def sel2():
        return as_bf16(col == (quad // 2) * block + dest * 2 + quad % 2)

    def sel1_t():
        return as_bf16(row_t == (quad_t % 2) * block + dest_t * 2 + quad_t // 2)

    def sel2_t():
        return as_bf16(row_t == (quad_t // 2) * block + dest_t * 2 + quad_t % 2)

    def diagonal(blocks):
        spread = as_bf16(iota((block, rows), 0) == iota((block, rows), 1) % block)
        wide = dot(blocks, spread)
        same = iota((rows, rows), 0) // block == iota((rows, rows), 1) // block
        return jnp.where(same, wide, 0.0).astype(BF16)

    def put_tall(ref, value):
        for c in range(CUTS):
            ref[:, c * rows : (c + 1) * rows] = jnp.where(cut_of == c, value, 0.0).astype(BF16)

    def put_flat(ref, value):
        for c in range(CUTS):
            ref[c * rows : (c + 1) * rows, :] = jnp.where(cut_of_t == c, value, 0.0).astype(BF16)

    def first_factor(at):
        put_tall(r.dfwd, dot(sel1(), diagonal(r.m1[at])))

    def factors(at):
        d1 = diagonal(r.m1[at])
        d2 = diagonal(r.m2[at])
        put_tall(r.dbwd.at[at], dot(sel2(), d2, 1, 1))
        put_flat(r.efwd, dot(d2, sel2_t()))
        put_flat(r.ebwd.at[at], dot(d1, sel1_t(), 0, 0))

    def norm(at):
        total = jnp.zeros((rows, LANES), F32)
        for _, _, t in tiles:
            v = r.x[at, :, t : t + LANES].astype(F32)
            total += v * v
        scale = lax.rsqrt(jnp.sum(total, axis=-1, keepdims=True) / width + 1e-06)
        scale = jnp.broadcast_to(scale, (rows, LANES))
        r.inv[at] = scale
        for f, c, t in tiles:
            v = r.x[at, :, t : t + LANES].astype(F32) * scale * r.gain[at, :, t : t + LANES]
            v = v.astype(BF16)
            r.nrm[:, t : t + LANES] = v
            r.nst[at, c * rows : (c + 1) * rows, f * LANES : (f + 1) * LANES] = v
        r.fsend[at] = dot(r.dfwd[...], r.nst[at]).astype(BF16)

    def forward(at):
        exchange(r.fsend.at[at], r.frecv.at[at], r.fs_sem.at[at], r.fr_sem.at[at], whole)

    def gate(at):
        for f in range(chunks):
            cols = slice(f * CHUNK, (f + 1) * CHUNK)
            pre = dot(r.nrm[...], r.wg[at, :, cols])
            s = jax.nn.sigmoid(pre)
            r.mf[at, :, cols] = pre * s
            r.gf[at, :, cols] = s * (1.0 + pre * (1.0 - s))

    def mixer(at):
        landed(r.frecv.at[at], r.fr_sem.at[at])
        mixed = dot(r.efwd[...], r.frecv[at])
        natural = dot(r.pick2[...], r.frecv[at]).astype(BF16)
        for f, c, t in tiles:
            part = (slice(c * rows, (c + 1) * rows), slice(f * LANES, (f + 1) * LANES))
            r.gf[at, :, t : t + LANES] = r.gf[at, :, t : t + LANES] * mixed[part]
            r.moved[at, :, t : t + LANES] = natural[part]

    @pl.when(worker)
    def _():
        loads[1].wait()
        first_factor(own)
        loads[0].wait()
        loads[3].wait()
        norm(own)

    pl.semaphore_wait(barrier, n_seq + n_pipe - 2)

    x_copy = remote(x_hbm, r.xnext, r.xs_sem, r.xr_sem, pipe_at(reader))
    x_sender = single | (plane == 3)
    there = jnp.where(plane == 1, 0, 1)

    def slab_at(flip_x, flip_y, j):
        unit = 4 * (1 - bit_x if flip_x else bit_x) + 2 * (1 - bit_y if flip_y else bit_y) + bit_c
        return pl.ds(pl.multiple_of((PIECES * unit + j) * slab, slab), slab)

    def supply():
        given = []
        for i, (src, dst) in enumerate(((wg_hbm, r.wg), (wo_hbm, r.wo))):
            for j in range(PIECES):
                at = slab_at(0, 0, j)
                given.append(
                    remote(
                        src.at[at],
                        dst.at[there, at],
                        r.ws_sem.at[i, j],
                        r.wz_sem.at[i, j],
                        pipe_at(mate),
                    )
                )
        small = [
            remote(src, dst.at[there], r.ps_sem.at[k], r.pr_sem.at[k], pipe_at(mate))
            for k, (src, dst) in enumerate(
                ((x_hbm, r.x), (m1_hbm, r.m1), (m2_hbm, r.m2), (gain_hbm, r.gain))
            )
        ]
        return small + given

    @pl.when(x_sender)
    def _():
        x_copy.start()

    @pl.when(supplier)
    def _():
        for copy in supply():
            copy.start()

    def weight(i):
        return r.wo if i else r.wg

    def piece(i, j, flip_x=0, flip_y=0):
        return weight(i).at[guest, slab_at(flip_x, flip_y, j)]

    def pass_own(i, j):
        ref = piece(i, j)
        return (
            remote(ref, ref, r.wxs_sem.at[i, j], r.wxr_sem.at[i, j], seq_at(x_mate(j))),
            remote(ref, ref, r.wys_sem.at[i, j], r.wyr_sem.at[i, j], seq_at(y_mate(j))),
            remote(ref, ref, r.wcs_sem.at[0, i, j], r.wc_sem.at[i], seq_at(core_mate)),
        )

    def pass_core(i, j, flip_x, flip_y):
        ref = piece(i, j, flip_x, flip_y)
        send_sem = r.wcs_sem.at[flip_x + 2 * flip_y, i, j]
        return remote(ref, ref, send_sem, r.wc_sem.at[i], seq_at(core_mate))

    def pass_corner(i, j, flip_x, flip_y):
        ref = piece(i, j, flip_x, flip_y)
        to = y_mate(j) if flip_x else x_mate(j)
        return remote(ref, ref, r.wds_sem.at[i, j], r.wdr_sem.at[i, j], seq_at(to))

    def collect_own(i, j):
        landed(piece(i, j), r.wz_sem.at[i, j])
        for copy in pass_own(i, j):
            copy.start()

    def collect_sides(i, j):
        landed(piece(i, j, 1, 0), r.wxr_sem.at[i, j])

        @pl.when(bit_c == 0)
        def _():
            pass_corner(i, j, 1, 0).start()

        pass_core(i, j, 1, 0).start()
        landed(piece(i, j, 0, 1), r.wyr_sem.at[i, j])

        @pl.when(bit_c == 1)
        def _():
            pass_corner(i, j, 0, 1).start()

        pass_core(i, j, 0, 1).start()

    def collect_corner(i, j):
        landed(piece(i, j, 1, 1), r.wdr_sem.at[i, j])
        pass_core(i, j, 1, 1).start()

    def collect_rest(i):
        landed(weight(i).at[guest, : width // 2], r.wc_sem.at[i])

    def finish_guest():
        for j in (PIECES - 2, PIECES - 1):
            collect_corner(1, j)
        collect_rest(1)

    @pl.when(worker)
    def _():
        forward(own)
        loads[2].wait()
        factors(own)
        put_flat(r.pick1, sel1_t().astype(F32))
        put_flat(r.pick2, sel2_t().astype(F32))
        loads[4].wait()
        gate(own)
        loads[5].wait()

    @pl.when(worker & jnp.logical_not(first))
    def _():
        mixer(own)

    def hidden_of(ref, at):
        for f in range(chunks):
            cols = slice(f * CHUNK, (f + 1) * CHUNK)
            r.xw[at, :, cols] = dot(ref[...], r.wo[at, cols, :], 1, 1)

    @pl.when(worker & jnp.logical_not(first))
    def _():
        x_copy.wait_recv()

    @pl.when(worker & jnp.logical_not(first) & jnp.logical_not(final))
    def _():
        hidden_of(r.xnext, 0)

    @pl.when(double)
    def _():
        for k, ref in enumerate((r.x, r.m1, r.m2, r.gain)):
            landed(ref.at[guest], r.pr_sem.at[k])
        first_factor(guest)
        factors(guest)
        norm(guest)
        forward(guest)
        steps = [(i, j) for i in range(2) for j in range(PIECES)]
        for t in range(len(steps) + 2):
            if t < len(steps):
                collect_own(*steps[t])
            if t >= 2:
                collect_sides(*steps[t - 2])
            if 3 <= t < len(steps) + 1:
                collect_corner(*steps[t - 3])
            if t == PIECES + 2:
                collect_rest(0)
                gate(guest)
                mixer(guest)

    @pl.when(double)
    def _():
        finish_guest()
        hidden_of(r.x.at[0], 1)

    @pl.when(final)
    def _():
        hidden_of(r.xnext, 0)

    @pl.when(first)
    def _():
        r.shift[...] = jnp.zeros(r.shift.shape, F32)
        r.xw[0] = jnp.zeros((rows, width), F32)
        r.xnext[...] = jnp.zeros(r.xnext.shape, BF16)

    eye = iota((rows, rows), 0) == iota((rows, rows), 1)
    c_copy = remote(r.csend, r.crecv, r.cs_sem, r.cr_sem, pipe_at(following))

    def hand(slot, f):
        return remote(
            r.abuf.at[slot + 1, f],
            r.abuf.at[0, f],
            r.zs_sem.at[f],
            r.zr_sem.at[f],
            pipe_at(following),
        )

    def partial(slot, k):
        deep = slice(k * CHUNK, (k + 1) * CHUNK)
        for f in range(chunks):
            cols = slice(f * CHUNK, (f + 1) * CHUNK)
            part = dot(r.abuf[slot, k], r.wo[slot, cols, deep], 1, 1)
            r.dh[:, cols] = part if k == 0 else r.dh[:, cols] + part

    def results(slot):
        inv = r.inv.at[slot]
        natural = dot(r.pick1[...], r.brecv[slot]).astype(BF16)
        sums = jnp.zeros((rows, rows), F32)
        for c in range(CUTS):
            part = slice(c * rows, (c + 1) * rows)
            sums += dot(natural[part, :], r.nst[slot, part, :], 1, 1)
        for a in range(2):
            r.r1[slot, a] = sums[a * block : (a + 1) * block, a * block : (a + 1) * block]

    def outgoing(slot):
        for _, _, t in tiles:
            cols = slice(t, t + LANES)
            r.res[slot, :, cols] = (
                r.anat[:, cols] - r.shift[...] * r.x[slot, :, cols].astype(F32)
            ).astype(BF16)

    def stores(slot):
        return [
            pltpu.make_async_copy(src.at[slot], dst, r.osem.at[k])
            for k, (src, dst) in enumerate(((r.res, out_hbm), (r.r1, g1_hbm), (r.r2, g2_hbm)))
        ]

    def returns(slot, kinds=range(3)):
        pairs = ((r.res, out_hbm), (r.r1, g1_hbm), (r.r2, g2_hbm))
        return [
            remote(
                pairs[k][0].at[slot], pairs[k][1], r.rs_sem.at[k], r.rr_sem.at[k], pipe_at(mate)
            )
            for k in kinds
        ]

    def chain(slot):
        if slot == 0:
            for k in range(chunks):
                cot_copy(k).wait()
                if k < chunks - 1:
                    partial(0, k)

            @pl.when(jnp.logical_not(first))
            def _():
                c_copy.wait_recv()
                spread = jnp.where(eye, jnp.broadcast_to(r.crecv[0:1, :], (rows, rows)), 0.0)
                r.shift[...] = jnp.broadcast_to(
                    jnp.sum(spread, axis=1, keepdims=True), r.shift.shape
                )

        k = chunks - 1
        deep = slice(k * CHUNK, (k + 1) * CHUNK)
        for f in range(chunks):
            cols = slice(f * CHUNK, (f + 1) * CHUNK)
            hidden = r.dh[:, cols] + dot(r.abuf[slot, k], r.wo[slot, cols, deep], 1, 1)
            hidden = hidden - r.shift[:, :1] * r.xw[slot, :, cols]
            r.dh[:, cols] = hidden
            mix = (hidden * r.mf[slot, :, cols]).astype(BF16)
            r.dmix[:, cols] = mix
            stack = jnp.concatenate(
                [mix[:, c * LANES : (c + 1) * LANES] for c in range(CUTS)], axis=0
            )
            lanes = slice(f * LANES, (f + 1) * LANES)
            r.bsend[slot, :, lanes] = dot(r.dbwd[slot], stack).astype(BF16)
            exchange(
                r.bsend.at[slot],
                r.brecv.at[slot],
                r.bs_sem.at[slot, f],
                r.br_sem.at[slot, f],
                lanes,
            )
        if slot == 0:

            @pl.when(first)
            def _():
                mixer(0)

        r.dgate[...] = (r.dh[...] * r.gf[slot]).astype(BF16)
        for f in range(chunks):
            cols = slice(f * CHUNK, (f + 1) * CHUNK)
            r.gb[:, cols] = dot(r.dgate[...], r.wg[slot, cols, :], 1, 1)
        g2 = dot(r.dmix[...], r.moved[slot], 1, 1)
        for a in range(2):
            r.r2[slot, a] = g2[a * block : (a + 1) * block, a * block : (a + 1) * block]
        if slot == 1:
            results(0)

            @pl.when(final)
            def _():
                for copy in returns(0, (1, 2)):
                    copy.start()

        sending = single if slot == 0 else jnp.logical_not(final)
        inv = r.inv.at[slot]
        total = jnp.zeros((rows, LANES), F32)
        for f in range(chunks):
            lanes = slice(f * LANES, (f + 1) * LANES)
            landed(r.brecv.at[slot, :, lanes], r.br_sem.at[slot, f])
            back = dot(r.ebwd[slot], r.brecv[slot, :, lanes])
            for c in range(CUTS):
                t = f * CHUNK + c * LANES
                cols = slice(t, t + LANES)
                delta = r.gain[slot, :, cols] * (back[c * rows : (c + 1) * rows, :] + r.gb[:, cols])
                unit = r.x[slot, :, cols].astype(F32) * inv[...]
                total += delta * unit
                here = slice(c * LANES, (c + 1) * LANES)
                prior = r.xnext[:, cols] if slot == 0 else r.x[0, :, cols]
                incoming = r.abuf[slot, f, :, here].astype(F32) - r.shift[...] * prior.astype(F32)
                value = incoming + inv[...] * delta
                r.anat[:, cols] = value
                r.abuf[slot + 1, f, :, here] = value.astype(BF16)
            if f < chunks - 1:

                @pl.when(sending)
                def _():
                    hand(slot, f).start()

                if slot == 0:

                    @pl.when(double)
                    def _():
                        partial(1, f)

        mean = jnp.sum(total, axis=-1, keepdims=True) / width
        fix = jnp.broadcast_to(mean, (rows, LANES)) * inv[...] * inv[...]

        @pl.when(sending)
        def _():
            line = jnp.sum(jnp.where(eye, fix[:, :1], 0.0), axis=0, keepdims=True)
            r.csend[...] = jnp.broadcast_to(line, r.csend.shape)
            c_copy.start()
            hand(slot, chunks - 1).start()

        r.shift[...] = fix
        outgoing(slot)
        if slot == 0:

            @pl.when(final)
            def _():
                returns(0, (0,))[0].start()

    @pl.when(worker)
    def _():
        chain(0)

    @pl.when(single)
    def _():
        results(0)

    @pl.when(double)
    def _():
        chain(1)
        results(1)

    @pl.when(double & jnp.logical_not(final))
    def _():
        c_copy.wait_send()
        for f in range(chunks):
            hand(1, f).wait_send()
        for copy in returns(1):
            copy.start()

    @pl.when(worker)
    def _():
        for copy in stores(own):
            copy.start()
        sent(r.fsend.at[own], r.fs_sem.at[own], whole)
        for f in range(chunks):
            sent(r.bsend.at[0], r.bs_sem.at[0, f], slice(f * LANES, (f + 1) * LANES))

    @pl.when(double)
    def _():
        sent(r.fsend.at[guest], r.fs_sem.at[guest], whole)
        for f in range(chunks):
            sent(r.bsend.at[1], r.bs_sem.at[1, f], slice(f * LANES, (f + 1) * LANES))
        for i in range(2):
            for j in range(PIECES):
                for copy in pass_own(i, j):
                    copy.wait_send()
                pass_core(i, j, 1, 0).wait_send()
                pass_core(i, j, 0, 1).wait_send()
                pass_core(i, j, 1, 1).wait_send()
                pass_corner(i, j, 1, 0).wait_send()
        for copy in returns(guest):
            copy.wait_send()

    @pl.when(x_sender)
    def _():
        x_copy.wait_send()

    @pl.when(single)
    def _():
        c_copy.wait_send()
        for f in range(chunks):
            hand(0, f).wait_send()

    @pl.when(supplier)
    def _():
        for copy in supply():
            copy.wait_send()
        for copy in returns(0):
            copy.wait_recv()

    @pl.when(worker)
    def _():
        for copy in stores(own):
            copy.wait()


def layers(n_seq, n_pipe, section_inputs, cotangent, gain, w_gate, w_out, mix_first, mix_second):
    _, rows, width = section_inputs.shape
    block = rows // 2
    chunks = width // CHUNK
    span = n_seq * PIECE
    dma = pltpu.SemaphoreType.DMA
    wide = chunks * LANES
    out, g1, g2 = pl.pallas_call(
        functools.partial(kernel, n_seq, n_pipe),
        out_shape=(
            jax.ShapeDtypeStruct((rows, width), BF16),
            jax.ShapeDtypeStruct((2, block, block), F32),
            jax.ShapeDtypeStruct((2, block, block), F32),
        ),
        in_specs=[pl.BlockSpec(memory_space=pl.ANY)] * 7,
        out_specs=(pl.BlockSpec(memory_space=pl.ANY),) * 3,
        scratch_shapes=[
            pltpu.VMEM((2, rows, width), BF16),
            pltpu.VMEM((2, 1, width), F32),
            pltpu.VMEM((2, width, width), BF16),
            pltpu.VMEM((2, width, width), BF16),
            pltpu.VMEM((2, rows, block), BF16),
            pltpu.VMEM((2, rows, block), BF16),
            pltpu.VMEM((rows, width), BF16),
            pltpu.VMEM((2, rows, width), F32),
            pltpu.VMEM((2, rows, LANES), F32),
            pltpu.VMEM((rows, LANES), F32),
            pltpu.VMEM((rows, width), BF16),
            pltpu.VMEM((2, span, wide), BF16),
            pltpu.VMEM((span, span), BF16),
            pltpu.VMEM((span, span), BF16),
            pltpu.VMEM((2, span, span), BF16),
            pltpu.VMEM((2, span, span), BF16),
            pltpu.VMEM((span, span), BF16),
            pltpu.VMEM((span, span), BF16),
            pltpu.VMEM((2, span, wide), BF16),
            pltpu.VMEM((2, span, wide), BF16),
            pltpu.VMEM((2, span, wide), BF16),
            pltpu.VMEM((2, span, wide), BF16),
            pltpu.VMEM((2, rows, width), BF16),
            pltpu.VMEM((2, rows, width), F32),
            pltpu.VMEM((2, rows, width), F32),
            pltpu.VMEM((rows, width), F32),
            pltpu.VMEM((rows, width), BF16),
            pltpu.VMEM((rows, width), BF16),
            pltpu.VMEM((rows, width), F32),
            pltpu.VMEM((rows, width), F32),
            pltpu.VMEM((3, chunks, rows, CHUNK), BF16),
            pltpu.VMEM((8, rows), F32),
            pltpu.VMEM((8, rows), F32),
            pltpu.VMEM((2, rows, width), BF16),
            pltpu.VMEM((2, 2, block, block), F32),
            pltpu.VMEM((2, 2, block, block), F32),
            dma((6,)),
            dma((3,)),
            dma,
            dma,
            dma((2,)),
            dma((2,)),
            dma((2, chunks)),
            dma((2, chunks)),
            dma((chunks,)),
            dma((chunks,)),
            dma,
            dma,
            dma((2, PIECES)),
            dma((2, PIECES)),
            dma((2, PIECES)),
            dma((2, PIECES)),
            dma((2, PIECES)),
            dma((2, PIECES)),
            dma((2, PIECES)),
            dma((2, PIECES)),
            dma((4, 2, PIECES)),
            dma((2,)),
            dma((4,)),
            dma((4,)),
            dma((3,)),
            dma((3,)),
        ],
        compiler_params=pltpu.CompilerParams(
            collective_id=0, has_side_effects=True, vmem_limit_bytes=60 * 1024 * 1024
        ),
    )(
        section_inputs[0],
        cotangent,
        gain,
        w_gate[0],
        w_out[0],
        mix_first[0].reshape(rows, block),
        mix_second[0].reshape(rows, block),
    )
    return out[None], g1[None], g2[None]


def solution(mesh):
    placed = (
        P("pipe", "seq", None),
        P("seq", None),
        P("pipe", None),
        P("pipe", None, None),
        P("pipe", None, None),
        P("pipe", "seq", None, None),
        P("pipe", "seq", None, None),
    )
    return jax.shard_map(
        functools.partial(layers, mesh.shape["seq"], mesh.shape["pipe"]),
        mesh=mesh,
        in_specs=placed,
        out_specs=(
            P("pipe", "seq", None),
            P("pipe", "seq", None, None),
            P("pipe", "seq", None, None),
        ),
        check_vma=False,
    )
```

```python
import functools

import jax
import jax.numpy as jnp
from jax import lax
from jax.experimental import pallas as pl
from jax.experimental.pallas import tpu as pltpu
from jax.sharding import PartitionSpec as P

MESH = pl.DeviceIdType.MESH
F32 = jnp.float32
BF16 = jnp.bfloat16
LANES = 128
CUTS = 4
CHUNK = LANES * CUTS
ROWS_TO = 4
PIECE = ROWS_TO * CUTS
PIECES = 4


def iota(shape, axis):
    return lax.broadcasted_iota(jnp.int32, shape, axis)


def dot(a, b, da=1, db=0):
    return lax.dot_general(a, b, (((da,), (db,)), ((), ())), preferred_element_type=F32)


def as_bf16(mask):
    return jnp.where(mask, 1.0, 0.0).astype(BF16)


SCRATCH = (
    "x", "gain", "wg", "wo", "m1", "m2", "xnext", "xw", "inv", "shift",
    "nrm", "nst", "dfwd", "efwd", "dbwd", "ebwd", "pick1", "pick2", "fsend", "frecv",
    "bsend", "brecv", "moved", "mf", "gf", "dh", "dmix", "dgate", "gb", "anat",
    "abuf", "csend", "crecv", "res", "r1", "r2", "lsem", "osem", "xs_sem", "xr_sem",
    "fs_sem", "fr_sem", "bs_sem", "br_sem", "zs_sem", "zr_sem", "cs_sem", "cr_sem", "ws_sem", "wz_sem", "wxs_sem", "wxr_sem", "wys_sem", "wyr_sem", "wds_sem", "wdr_sem", "wcs_sem", "wc_sem", "ps_sem", "pr_sem", "rs_sem", "rr_sem",
)


class Refs:
    pass


def kernel(
    n_seq, n_pipe, x_hbm, cot_hbm, gain_hbm, wg_hbm, wo_hbm, m1_hbm, m2_hbm, out_hbm, g1_hbm, g2_hbm, *scratch
):
    r = Refs()
    for name, ref in zip(SCRATCH, scratch, strict=True):
        setattr(r, name, ref)
    me = lax.axis_index("seq")
    plane = lax.axis_index("pipe")
    _, rows, width = r.x.shape
    block = rows // 2
    chunks = width // CHUNK
    span = n_seq * PIECE
    whole = slice(0, chunks * LANES)
    tiles = [(f, c, (f * CUTS + c) * LANES) for f in range(chunks) for c in range(CUTS)]

    first = plane == 7
    final = plane == 0
    double = (plane == 4) | final
    supplier = (plane == 3) | (plane == 1)
    worker = jnp.logical_not(supplier)
    single = worker & jnp.logical_not(double)
    mate = jnp.where(plane >= 3, 7 - plane, 1 - plane)
    own = jnp.where(final, 1, 0)
    guest = 1 - own
    before = lax.rem(plane + n_pipe - 1, n_pipe)
    following = jnp.where(plane == 4, 2, jnp.where(plane == 2, 0, before))
    reader = jnp.where(plane == 2, 0, before)
    far = 8 if n_seq == 32 else 4
    bit_x, bit_y, bit_c = (me // far) % 2, (me // 2) % 2, me % 2
    n_x, n_y = n_seq // far, far // 2
    at_x, at_y = me // far, (me // 2) % n_y

    def across(place, bit, count, j):
        step = 1 - 2 * bit if j % 2 == 0 else 2 * bit - 1
        return lax.rem(place + step + count, count)

    def x_mate(j):
        return me + far * (across(at_x, bit_x, n_x, j) - at_x)

    def y_mate(j):
        return me + 2 * (across(at_y, bit_y, n_y, j) - at_y)

    core_mate = me + 1 - 2 * bit_c
    slab = width // (8 * PIECES)

    def seq_at(device):
        return {"seq": device}

    def pipe_at(device):
        return {"pipe": device}

    def remote(src, dst, send_sem, recv_sem, device):
        return pltpu.make_async_remote_copy(
            src_ref=src,
            dst_ref=dst,
            send_sem=send_sem,
            recv_sem=recv_sem,
            device_id=device,
            device_id_type=MESH,
        )

    def landed(ref, sem):
        pltpu.make_async_copy(ref, ref, sem).wait()

    loads = [
        pltpu.make_async_copy(src, dst, r.lsem.at[i])
        for i, (src, dst) in enumerate(
            (
                (x_hbm, r.x.at[own]),
                (m1_hbm, r.m1.at[own]),
                (m2_hbm, r.m2.at[own]),
                (gain_hbm, r.gain.at[own]),
                (wg_hbm, r.wg.at[own]),
                (wo_hbm, r.wo.at[own]),
            )
        )
    ]

    @pl.when(worker)
    def _():
        for copy in loads:
            copy.start()

    def cot_copy(f):
        return pltpu.make_async_copy(
            cot_hbm.at[:, f * CHUNK : (f + 1) * CHUNK], r.abuf.at[0, f], r.zr_sem.at[f]
        )

    @pl.when(first)
    def _():
        for f in range(chunks):
            cot_copy(f).start()

    barrier = pltpu.get_barrier_semaphore()

    @pl.loop(1, n_seq)
    def _(i):
        pl.semaphore_signal(
            barrier, inc=1, device_id=seq_at(lax.rem(me + i, n_seq)), device_id_type=MESH
        )

    @pl.loop(1, n_pipe)
    def _(i):
        pl.semaphore_signal(
            barrier, inc=1, device_id=pipe_at(lax.rem(plane + i, n_pipe)), device_id_type=MESH
        )

    places_x = [lax.rem(at_x + d, n_x) for d in range(n_x)]
    places_y = [lax.rem(at_y + d, n_y) for d in range(n_y)]
    places_c = [bit_c, 1 - bit_c]
    others = sorted(
        ((dx, dy, dc) for dx in range(n_x) for dy in range(n_y) for dc in range(2) if dx or dy or dc),
        key=lambda d: -3 * (min(d[0], n_x - d[0]) + min(d[1], n_y - d[1])) - d[2],
    )

    def exchange(send, recv, send_sem, recv_sem, lanes):
        mine = pl.ds(pl.multiple_of(me * PIECE, PIECE), PIECE)
        pltpu.make_async_copy(send.at[mine, lanes], recv.at[mine, lanes], recv_sem).start()

        for dx, dy, dc in others:
            to = far * places_x[dx] + 2 * places_y[dy] + places_c[dc]
            theirs = pl.ds(pl.multiple_of(to * PIECE, PIECE), PIECE)
            remote(send.at[theirs, lanes], recv.at[mine, lanes], send_sem, recv_sem, seq_at(to)).start()

    def sent(send, send_sem, lanes):
        landed(send.at[: span - PIECE, lanes], send_sem)

    spot = iota((span, rows), 0)
    col = iota((span, rows), 1)
    dest = spot // PIECE
    quad = spot % ROWS_TO
    cut_of = (spot // ROWS_TO) % CUTS
    spot_t = iota((rows, span), 1)
    row_t = iota((rows, span), 0)
    dest_t = spot_t // PIECE
    quad_t = spot_t % ROWS_TO
    cut_of_t = (spot_t // ROWS_TO) % CUTS

    def sel1():
        return as_bf16(col == (quad % 2) * block + dest * 2 + quad // 2)

    def sel2():
        return as_bf16(col == (quad // 2) * block + dest * 2 + quad % 2)

    def sel1_t():
        return as_bf16(row_t == (quad_t % 2) * block + dest_t * 2 + quad_t // 2)

    def sel2_t():
        return as_bf16(row_t == (quad_t // 2) * block + dest_t * 2 + quad_t % 2)

    def diagonal(blocks):
        spread = as_bf16(iota((block, rows), 0) == iota((block, rows), 1) % block)
        wide = dot(blocks, spread)
        same = iota((rows, rows), 0) // block == iota((rows, rows), 1) // block
        return jnp.where(same, wide, 0.0).astype(BF16)

    def put_tall(ref, value):
        for c in range(CUTS):
            ref[:, c * rows : (c + 1) * rows] = jnp.where(cut_of == c, value, 0.0).astype(BF16)

    def put_flat(ref, value):
        for c in range(CUTS):
            ref[c * rows : (c + 1) * rows, :] = jnp.where(cut_of_t == c, value, 0.0).astype(BF16)

    def first_factor(at):
        put_tall(r.dfwd, dot(sel1(), diagonal(r.m1[at])))

    def factors(at):
        d1 = diagonal(r.m1[at])
        d2 = diagonal(r.m2[at])
        put_tall(r.dbwd.at[at], dot(sel2(), d2, 1, 1))
        put_flat(r.efwd, dot(d2, sel2_t()))
        put_flat(r.ebwd.at[at], dot(d1, sel1_t(), 0, 0))

    def norm(at):
        total = jnp.zeros((rows, LANES), F32)
        for _, _, t in tiles:
            v = r.x[at, :, t : t + LANES].astype(F32)
            total += v * v
        scale = lax.rsqrt(jnp.sum(total, axis=-1, keepdims=True) / width + 1e-06)
        scale = jnp.broadcast_to(scale, (rows, LANES))
        r.inv[at] = scale
        for f, c, t in tiles:
            v = r.x[at, :, t : t + LANES].astype(F32) * scale * r.gain[at, :, t : t + LANES]
            v = v.astype(BF16)
            r.nrm[:, t : t + LANES] = v
            r.nst[at, c * rows : (c + 1) * rows, f * LANES : (f + 1) * LANES] = v
        r.fsend[at] = dot(r.dfwd[...], r.nst[at]).astype(BF16)

    def forward(at):
        exchange(r.fsend.at[at], r.frecv.at[at], r.fs_sem.at[at], r.fr_sem.at[at], whole)

    def gate(at):
        for f in range(chunks):
            cols = slice(f * CHUNK, (f + 1) * CHUNK)
            pre = dot(r.nrm[...], r.wg[at, :, cols])
            s = jax.nn.sigmoid(pre)
            r.mf[at, :, cols] = pre * s
            r.gf[at, :, cols] = s * (1.0 + pre * (1.0 - s))

    def mixer(at):
        landed(r.frecv.at[at], r.fr_sem.at[at])
        mixed = dot(r.efwd[...], r.frecv[at])
        natural = dot(r.pick2[...], r.frecv[at]).astype(BF16)
        for f, c, t in tiles:
            part = (slice(c * rows, (c + 1) * rows), slice(f * LANES, (f + 1) * LANES))
            r.gf[at, :, t : t + LANES] = r.gf[at, :, t : t + LANES] * mixed[part]
            r.moved[at, :, t : t + LANES] = natural[part]

    @pl.when(worker)
    def _():
        loads[1].wait()
        first_factor(own)
        loads[0].wait()
        loads[3].wait()
        norm(own)

    pl.semaphore_wait(barrier, n_seq + n_pipe - 2)

    x_copy = remote(x_hbm, r.xnext, r.xs_sem, r.xr_sem, pipe_at(reader))
    x_sender = single | (plane == 3)
    there = jnp.where(plane == 1, 0, 1)

    def slab_at(flip_x, flip_y, j):
        unit = 4 * (1 - bit_x if flip_x else bit_x) + 2 * (1 - bit_y if flip_y else bit_y) + bit_c
        return pl.ds(pl.multiple_of((PIECES * unit + j) * slab, slab), slab)

    def supply():
        given = []
        for i, (src, dst) in enumerate(((wg_hbm, r.wg), (wo_hbm, r.wo))):
            for j in range(PIECES):
                at = slab_at(0, 0, j)
                given.append(
                    remote(
                        src.at[at],
                        dst.at[there, at],
                        r.ws_sem.at[i, j],
                        r.wz_sem.at[i, j],
                        pipe_at(mate),
                    )
                )
        small = [
            remote(src, dst.at[there], r.ps_sem.at[k], r.pr_sem.at[k], pipe_at(mate))
            for k, (src, dst) in enumerate(
                ((x_hbm, r.x), (m1_hbm, r.m1), (m2_hbm, r.m2), (gain_hbm, r.gain))
            )
        ]
        return small + given

    @pl.when(x_sender)
    def _():
        x_copy.start()

    @pl.when(supplier)
    def _():
        for copy in supply():
            copy.start()

    def weight(i):
        return r.wo if i else r.wg

    def piece(i, j, flip_x=0, flip_y=0):
        return weight(i).at[guest, slab_at(flip_x, flip_y, j)]

    def pass_own(i, j):
        ref = piece(i, j)
        return (
            remote(ref, ref, r.wxs_sem.at[i, j], r.wxr_sem.at[i, j], seq_at(x_mate(j))),
            remote(ref, ref, r.wys_sem.at[i, j], r.wyr_sem.at[i, j], seq_at(y_mate(j))),
            remote(ref, ref, r.wcs_sem.at[0, i, j], r.wc_sem.at[i], seq_at(core_mate)),
        )

    def pass_core(i, j, flip_x, flip_y):
        ref = piece(i, j, flip_x, flip_y)
        send_sem = r.wcs_sem.at[flip_x + 2 * flip_y, i, j]
        return remote(ref, ref, send_sem, r.wc_sem.at[i], seq_at(core_mate))

    def pass_corner(i, j, flip_x, flip_y):
        ref = piece(i, j, flip_x, flip_y)
        to = y_mate(j) if flip_x else x_mate(j)
        return remote(ref, ref, r.wds_sem.at[i, j], r.wdr_sem.at[i, j], seq_at(to))

    def collect_own(i, j):
        landed(piece(i, j), r.wz_sem.at[i, j])
        for copy in pass_own(i, j):
            copy.start()

    def collect_sides(i, j):
        landed(piece(i, j, 1, 0), r.wxr_sem.at[i, j])

        @pl.when(bit_c == 0)
        def _():
            pass_corner(i, j, 1, 0).start()

        pass_core(i, j, 1, 0).start()
        landed(piece(i, j, 0, 1), r.wyr_sem.at[i, j])

        @pl.when(bit_c == 1)
        def _():
            pass_corner(i, j, 0, 1).start()

        pass_core(i, j, 0, 1).start()

    def collect_corner(i, j):
        landed(piece(i, j, 1, 1), r.wdr_sem.at[i, j])
        pass_core(i, j, 1, 1).start()

    def collect_rest(i):
        landed(weight(i).at[guest, : width // 2], r.wc_sem.at[i])

    def finish_guest():
        for j in (PIECES - 2, PIECES - 1):
            collect_corner(1, j)
        collect_rest(1)

    @pl.when(worker)
    def _():
        forward(own)
        loads[2].wait()
        factors(own)
        put_flat(r.pick1, sel1_t().astype(F32))
        put_flat(r.pick2, sel2_t().astype(F32))
        loads[4].wait()
        gate(own)
        loads[5].wait()

    @pl.when(worker & jnp.logical_not(first))
    def _():
        mixer(own)

    def hidden_of(ref, at):
        for f in range(chunks):
            cols = slice(f * CHUNK, (f + 1) * CHUNK)
            r.xw[at, :, cols] = dot(ref[...], r.wo[at, cols, :], 1, 1)

    @pl.when(worker & jnp.logical_not(first))
    def _():
        x_copy.wait_recv()

    @pl.when(worker & jnp.logical_not(first) & jnp.logical_not(final))
    def _():
        hidden_of(r.xnext, 0)

    @pl.when(double)
    def _():
        for k, ref in enumerate((r.x, r.m1, r.m2, r.gain)):
            landed(ref.at[guest], r.pr_sem.at[k])
        first_factor(guest)
        factors(guest)
        norm(guest)
        forward(guest)
        steps = [(i, j) for i in range(2) for j in range(PIECES)]
        for t in range(len(steps) + 2):
            if t < len(steps):
                collect_own(*steps[t])
            if t >= 2:
                collect_sides(*steps[t - 2])
            if 3 <= t < len(steps) + 1:
                collect_corner(*steps[t - 3])
            if t == PIECES + 2:
                collect_rest(0)
                gate(guest)
                mixer(guest)

    @pl.when(double)
    def _():
        finish_guest()
        hidden_of(r.x.at[0], 1)

    @pl.when(final)
    def _():
        hidden_of(r.xnext, 0)

    @pl.when(first)
    def _():
        r.shift[...] = jnp.zeros(r.shift.shape, F32)
        r.xw[0] = jnp.zeros((rows, width), F32)
        r.xnext[...] = jnp.zeros(r.xnext.shape, BF16)

    eye = iota((rows, rows), 0) == iota((rows, rows), 1)
    c_copy = remote(r.csend, r.crecv, r.cs_sem, r.cr_sem, pipe_at(following))

    def hand(slot, f):
        return remote(
            r.abuf.at[slot + 1, f],
            r.abuf.at[0, f],
            r.zs_sem.at[f],
            r.zr_sem.at[f],
            pipe_at(following),
        )

    def partial(slot, k):
        deep = slice(k * CHUNK, (k + 1) * CHUNK)
        for f in range(chunks):
            cols = slice(f * CHUNK, (f + 1) * CHUNK)
            part = dot(r.abuf[slot, k], r.wo[slot, cols, deep], 1, 1)
            r.dh[:, cols] = part if k == 0 else r.dh[:, cols] + part

    def results(slot):
        inv = r.inv.at[slot]
        natural = dot(r.pick1[...], r.brecv[slot]).astype(BF16)
        sums = jnp.zeros((rows, rows), F32)
        for c in range(CUTS):
            part = slice(c * rows, (c + 1) * rows)
            sums += dot(natural[part, :], r.nst[slot, part, :], 1, 1)
        for a in range(2):
            r.r1[slot, a] = sums[a * block : (a + 1) * block, a * block : (a + 1) * block]

    def outgoing(slot):
        for _, _, t in tiles:
            cols = slice(t, t + LANES)
            r.res[slot, :, cols] = (
                r.anat[:, cols] - r.shift[...] * r.x[slot, :, cols].astype(F32)
            ).astype(BF16)

    def stores(slot, kinds=range(3)):
        pairs = ((r.res, out_hbm), (r.r1, g1_hbm), (r.r2, g2_hbm))
        return [
            pltpu.make_async_copy(pairs[k][0].at[slot], pairs[k][1], r.osem.at[k]) for k in kinds
        ]

    def returns(slot, kinds=range(3)):
        pairs = ((r.res, out_hbm), (r.r1, g1_hbm), (r.r2, g2_hbm))
        return [
            remote(
                pairs[k][0].at[slot], pairs[k][1], r.rs_sem.at[k], r.rr_sem.at[k], pipe_at(mate)
            )
            for k in kinds
        ]

    def chain(slot):
        if slot == 0:
            for k in range(chunks):
                cot_copy(k).wait()
                if k < chunks - 1:
                    partial(0, k)

            @pl.when(jnp.logical_not(first))
            def _():
                c_copy.wait_recv()
                spread = jnp.where(eye, jnp.broadcast_to(r.crecv[0:1, :], (rows, rows)), 0.0)
                r.shift[...] = jnp.broadcast_to(
                    jnp.sum(spread, axis=1, keepdims=True), r.shift.shape
                )

        k = chunks - 1
        deep = slice(k * CHUNK, (k + 1) * CHUNK)
        for f in range(chunks):
            cols = slice(f * CHUNK, (f + 1) * CHUNK)
            hidden = r.dh[:, cols] + dot(r.abuf[slot, k], r.wo[slot, cols, deep], 1, 1)
            hidden = hidden - r.shift[:, :1] * r.xw[slot, :, cols]
            r.dh[:, cols] = hidden
            mix = (hidden * r.mf[slot, :, cols]).astype(BF16)
            r.dmix[:, cols] = mix
            stack = jnp.concatenate(
                [mix[:, c * LANES : (c + 1) * LANES] for c in range(CUTS)], axis=0
            )
            lanes = slice(f * LANES, (f + 1) * LANES)
            r.bsend[slot, :, lanes] = dot(r.dbwd[slot], stack).astype(BF16)
            exchange(
                r.bsend.at[slot],
                r.brecv.at[slot],
                r.bs_sem.at[slot, f],
                r.br_sem.at[slot, f],
                lanes,
            )
        if slot == 0:

            @pl.when(first)
            def _():
                mixer(0)

        r.dgate[...] = (r.dh[...] * r.gf[slot]).astype(BF16)
        for f in range(chunks):
            cols = slice(f * CHUNK, (f + 1) * CHUNK)
            r.gb[:, cols] = dot(r.dgate[...], r.wg[slot, cols, :], 1, 1)
        g2 = dot(r.dmix[...], r.moved[slot], 1, 1)
        for a in range(2):
            r.r2[slot, a] = g2[a * block : (a + 1) * block, a * block : (a + 1) * block]
        if slot == 1:
            results(0)

            @pl.when(final)
            def _():
                for copy in returns(0, (1, 2)):
                    copy.start()

        sending = single if slot == 0 else jnp.logical_not(final)
        inv = r.inv.at[slot]
        total = jnp.zeros((rows, LANES), F32)
        for f in range(chunks):
            lanes = slice(f * LANES, (f + 1) * LANES)
            landed(r.brecv.at[slot, :, lanes], r.br_sem.at[slot, f])
            back = dot(r.ebwd[slot], r.brecv[slot, :, lanes])
            for c in range(CUTS):
                t = f * CHUNK + c * LANES
                cols = slice(t, t + LANES)
                delta = r.gain[slot, :, cols] * (back[c * rows : (c + 1) * rows, :] + r.gb[:, cols])
                unit = r.x[slot, :, cols].astype(F32) * inv[...]
                total += delta * unit
                here = slice(c * LANES, (c + 1) * LANES)
                prior = r.xnext[:, cols] if slot == 0 else r.x[0, :, cols]
                incoming = r.abuf[slot, f, :, here].astype(F32) - r.shift[...] * prior.astype(F32)
                value = incoming + inv[...] * delta
                r.anat[:, cols] = value
                r.abuf[slot + 1, f, :, here] = value.astype(BF16)
            if f < chunks - 1:

                @pl.when(sending)
                def _():
                    hand(slot, f).start()

                if slot == 0:

                    @pl.when(double)
                    def _():
                        partial(1, f)

        mean = jnp.sum(total, axis=-1, keepdims=True) / width
        fix = jnp.broadcast_to(mean, (rows, LANES)) * inv[...] * inv[...]

        @pl.when(sending)
        def _():
            line = jnp.sum(jnp.where(eye, fix[:, :1], 0.0), axis=0, keepdims=True)
            r.csend[...] = jnp.broadcast_to(line, r.csend.shape)
            c_copy.start()
            hand(slot, chunks - 1).start()

        r.shift[...] = fix
        outgoing(slot)
        if slot == 0:

            @pl.when(final)
            def _():
                returns(0, (0,))[0].start()

    @pl.when(worker)
    def _():
        chain(0)

    @pl.when(single)
    def _():
        results(0)

    @pl.when(double)
    def _():
        chain(1)

        @pl.when(final)
        def _():
            stores(own, (0,))[0].start()

        results(1)

    @pl.when(double & jnp.logical_not(final))
    def _():
        c_copy.wait_send()
        for f in range(chunks):
            hand(1, f).wait_send()
        for copy in returns(1):
            copy.start()

    @pl.when(worker & jnp.logical_not(final))
    def _():
        stores(own, (0,))[0].start()

    @pl.when(worker)
    def _():
        for copy in stores(own, (1, 2)):
            copy.start()
        sent(r.fsend.at[own], r.fs_sem.at[own], whole)
        for f in range(chunks):
            sent(r.bsend.at[0], r.bs_sem.at[0, f], slice(f * LANES, (f + 1) * LANES))

    @pl.when(double)
    def _():
        sent(r.fsend.at[guest], r.fs_sem.at[guest], whole)
        for f in range(chunks):
            sent(r.bsend.at[1], r.bs_sem.at[1, f], slice(f * LANES, (f + 1) * LANES))
        for i in range(2):
            for j in range(PIECES):
                for copy in pass_own(i, j):
                    copy.wait_send()
                pass_core(i, j, 1, 0).wait_send()
                pass_core(i, j, 0, 1).wait_send()
                pass_core(i, j, 1, 1).wait_send()
                pass_corner(i, j, 1, 0).wait_send()
        for copy in returns(guest):
            copy.wait_send()

    @pl.when(x_sender)
    def _():
        x_copy.wait_send()

    @pl.when(single)
    def _():
        c_copy.wait_send()
        for f in range(chunks):
            hand(0, f).wait_send()

    @pl.when(supplier)
    def _():
        for copy in supply():
            copy.wait_send()
        for copy in returns(0):
            copy.wait_recv()

    @pl.when(worker)
    def _():
        for copy in stores(own):
            copy.wait()


def layers(n_seq, n_pipe, section_inputs, cotangent, gain, w_gate, w_out, mix_first, mix_second):
    _, rows, width = section_inputs.shape
    block = rows // 2
    chunks = width // CHUNK
    span = n_seq * PIECE
    dma = pltpu.SemaphoreType.DMA
    wide = chunks * LANES
    out, g1, g2 = pl.pallas_call(
        functools.partial(kernel, n_seq, n_pipe),
        out_shape=(
            jax.ShapeDtypeStruct((rows, width), BF16),
            jax.ShapeDtypeStruct((2, block, block), F32),
            jax.ShapeDtypeStruct((2, block, block), F32),
        ),
        in_specs=[pl.BlockSpec(memory_space=pl.ANY)] * 7,
        out_specs=(pl.BlockSpec(memory_space=pl.ANY),) * 3,
        scratch_shapes=[
            pltpu.VMEM((2, rows, width), BF16),
            pltpu.VMEM((2, 1, width), F32),
            pltpu.VMEM((2, width, width), BF16),
            pltpu.VMEM((2, width, width), BF16),
            pltpu.VMEM((2, rows, block), BF16),
            pltpu.VMEM((2, rows, block), BF16),
            pltpu.VMEM((rows, width), BF16),
            pltpu.VMEM((2, rows, width), F32),
            pltpu.VMEM((2, rows, LANES), F32),
            pltpu.VMEM((rows, LANES), F32),
            pltpu.VMEM((rows, width), BF16),
            pltpu.VMEM((2, span, wide), BF16),
            pltpu.VMEM((span, span), BF16),
            pltpu.VMEM((span, span), BF16),
            pltpu.VMEM((2, span, span), BF16),
            pltpu.VMEM((2, span, span), BF16),
            pltpu.VMEM((span, span), BF16),
            pltpu.VMEM((span, span), BF16),
            pltpu.VMEM((2, span, wide), BF16),
            pltpu.VMEM((2, span, wide), BF16),
            pltpu.VMEM((2, span, wide), BF16),
            pltpu.VMEM((2, span, wide), BF16),
            pltpu.VMEM((2, rows, width), BF16),
            pltpu.VMEM((2, rows, width), F32),
            pltpu.VMEM((2, rows, width), F32),
            pltpu.VMEM((rows, width), F32),
            pltpu.VMEM((rows, width), BF16),
            pltpu.VMEM((rows, width), BF16),
            pltpu.VMEM((rows, width), F32),
            pltpu.VMEM((rows, width), F32),
            pltpu.VMEM((3, chunks, rows, CHUNK), BF16),
            pltpu.VMEM((8, rows), F32),
            pltpu.VMEM((8, rows), F32),
            pltpu.VMEM((2, rows, width), BF16),
            pltpu.VMEM((2, 2, block, block), F32),
            pltpu.VMEM((2, 2, block, block), F32),
            dma((6,)),
            dma((3,)),
            dma,
            dma,
            dma((2,)),
            dma((2,)),
            dma((2, chunks)),
            dma((2, chunks)),
            dma((chunks,)),
            dma((chunks,)),
            dma,
            dma,
            dma((2, PIECES)),
            dma((2, PIECES)),
            dma((2, PIECES)),
            dma((2, PIECES)),
            dma((2, PIECES)),
            dma((2, PIECES)),
            dma((2, PIECES)),
            dma((2, PIECES)),
            dma((4, 2, PIECES)),
            dma((2,)),
            dma((4,)),
            dma((4,)),
            dma((3,)),
            dma((3,)),
        ],
        compiler_params=pltpu.CompilerParams(
            collective_id=0, has_side_effects=True, vmem_limit_bytes=60 * 1024 * 1024
        ),
    )(
        section_inputs[0],
        cotangent,
        gain,
        w_gate[0],
        w_out[0],
        mix_first[0].reshape(rows, block),
        mix_second[0].reshape(rows, block),
    )
    return out[None], g1[None], g2[None]


def solution(mesh):
    placed = (
        P("pipe", "seq", None),
        P("seq", None),
        P("pipe", None),
        P("pipe", None, None),
        P("pipe", None, None),
        P("pipe", "seq", None, None),
        P("pipe", "seq", None, None),
    )
    return jax.shard_map(
        functools.partial(layers, mesh.shape["seq"], mesh.shape["pipe"]),
        mesh=mesh,
        in_specs=placed,
        out_specs=(
            P("pipe", "seq", None),
            P("pipe", "seq", None, None),
            P("pipe", "seq", None, None),
        ),
        check_vma=False,
    )
```
